1024 devices in a mesh: section: 128 (over y, z_hi, x), tensor: 8 (over z_lo, core).
Axes of the slice: x: 8, y: 8, z: 8 (z_hi: 2, z_lo: 4; z = z_hi * 4 + z_lo), core: 2. Of those that a mesh axis runs over, the one named last changes fastest.
Arguments:
- produced: bfloat16 [128, 2, 192, 8192], P('section', None, None, 'tensor'), may hold values from -7 to 7
- saved_inputs: bfloat16 [128, 192, 8192], P('section', None, 'tensor'), may hold values from -7 to 7
- upstream: bfloat16 [128, 192, 8192], P('section', None, 'tensor'), may hold values from -6 to 6
- norm_gain: float32 [128, 8192], P('section', 'tensor'), may hold values from 0.1 to 1.9
- w_key: bfloat16 [128, 8, 1024, 128], P('section', 'tensor'), may hold values from -22 to 22
- w_value: bfloat16 [128, 8, 1024, 128], P('section', 'tensor'), may hold values from -0.1875 to 0.1875
- batch_order: int32 [128], replicated, may hold values from 0 to 1
- segment_ids: int32 [2, 192], replicated, may hold values from 0 to 3, never falling along the last dimension, each value on 1 to 96 neighbouring positions
Outputs:
- forward_out: bfloat16 [128, 192, 8192], P('section', None, 'tensor')
- input_grad: bfloat16 [128, 192, 8192], P('section', None, 'tensor')
The draws below stay inside these ranges and needn't reach their ends.
Inputs may be any that keep to these rules, and one draw needn't show every extreme that they name: `segment_ids`: each row numbers the documents of one micro-batch in order; a document's tokens are contiguous.
All inputs are finite; a program needn't handle non-finite values.
Results may differ from the reference program's by a relative error of at most 0.0055.
The reference program's roundings to bfloat16 on the way count: a program that leaves them out, or rounds other values in their place, can miss the bound.
Values may be sent and summed in bfloat16 or wider, within the bound.
A program may use at most 32 MiB of HBM per device.

```python
import math
import jax
import jax.numpy as jnp
import numpy as np
from jax import lax

D = 8192
KV_HEADS = 8
HEAD_DIM = 128
SEQ = 192
GROUP = 8
SECTIONS = 128


def column_scale(width):
    return 0.75 * 3.0 ** (0.5 * jnp.arange(width, dtype=jnp.float32) / width)


def make_stream(key, shape):
    first = jax.random.fold_in(key, 0)
    columns = column_scale(shape[-1])
    values = jnp.clip(jax.random.normal(first, shape, jnp.float32), -4.0, 4.0)
    return (values * columns).astype(jnp.bfloat16)


def draw_produced(key, part):
    return make_stream(jax.random.fold_in(key, 11), (SECTIONS, 2, SEQ, D))


def draw_saved_inputs(key, part):
    return make_stream(jax.random.fold_in(key, 23), (SECTIONS, SEQ, D))


def draw_w_key(key, part):
    first = jax.random.fold_in(jax.random.fold_in(key, 37), 0)
    fan_in = GROUP * HEAD_DIM
    noise = jnp.clip(jax.random.normal(first, (SECTIONS, KV_HEADS, fan_in, HEAD_DIM), jnp.float32), -4.0, 4.0) / jnp.sqrt(1.0 * fan_in)
    return noise.astype(jnp.bfloat16)


def touch_ends(result, key, least, top_value):
    dims = result.shape
    place = [jax.random.randint(jax.random.fold_in(key, axis), (), 0, dims[axis]) for axis in range(len(dims))]
    result = result.at[tuple(place)].set(least)
    longest = dims.index(max(dims))
    place[longest] = (place[longest] + 1) % dims[longest]
    return result.at[tuple(place)].set(top_value)


def steps_of(own_key, dims, pieces, smallest, largest):
    gain = 1.0
    for dim, blocks in pieces:
        steps = jax.random.uniform(jax.random.fold_in(jax.random.fold_in(own_key, 6), dim), (blocks,), jnp.float32, smallest / len(pieces), largest / len(pieces))
        gain = gain * jnp.repeat(jnp.exp(steps), dims[dim] // blocks).reshape((-1,) + (1,) * (len(dims) - 1 - dim))
    return gain


def length_profile(number_of, total, reach, skew):
    weights = [(1 << 20) // math.isqrt(grade ** skew) + 1 for grade in range(2, number_of + 1)]
    rest, given = total - reach - (number_of - 1), [1] * (number_of - 1)
    while rest > 0:
        free = [i for i in range(number_of - 1) if given[i] < reach]
        whole, remaining = sum([weights[i] for i in free]), rest
        for i in free:
            extra = min(reach - given[i], max(1, remaining * weights[i] // whole), rest)
            given[i] = given[i] + extra
            rest = rest - extra
    return np.array([reach] + given)


def uneven_parts(stream_key, amount, total, limit, lean):
    if amount == 2:
        one = jax.random.randint(stream_key, (), max(1, total - limit), min(limit, total - 1) + 1)
        return jnp.stack([one, total - one])
    lengths = jnp.asarray(length_profile(amount, total, limit, lean), jnp.int32)
    pairs = (amount - 1) // 2
    source_of, taker = lengths[1:1 + 2 * pairs:2], lengths[2:2 + 2 * pairs:2]
    margin = jnp.minimum(source_of - 1, limit - taker)
    passed = jax.random.randint(jax.random.fold_in(stream_key, 1), (pairs,), 0, 1 << 20) % (margin + 1)
    lengths = lengths.at[1:1 + 2 * pairs:2].set(source_of - passed).at[2:2 + 2 * pairs:2].set(taker + passed)
    return lengths[jax.random.permutation(jax.random.fold_in(stream_key, 2), amount)]


def normal_values(stream_key, extent, scale, most, shards=(), held_as=jnp.bfloat16):
    level = steps_of(stream_key, extent, shards, -0.22, 0.18) if shards else 1.0
    array = jax.random.normal(stream_key, extent, jnp.float32) * scale * level
    return jnp.minimum(jnp.maximum(array, -most), most).astype(held_as)


def setup_inputs(seed: int = 0) -> dict:
    key_of = jax.random.split(jax.random.key(seed), 9)
    return {
        "produced": draw_produced(jax.random.fold_in(key_of[8], 71), 0),
        "saved_inputs": draw_saved_inputs(jax.random.fold_in(key_of[8], 71), 0),
        "upstream": normal_values(key_of[2], (SECTIONS, SEQ, D), 1.0, 6.0, ((0, 128), (2, 8))),
        "norm_gain": jnp.clip(1.0 + 0.18 * jax.random.normal(key_of[3], (SECTIONS, D), jnp.float32), 0.1, 1.9),
        "w_key": draw_w_key(jax.random.fold_in(key_of[8], 71), 0),
        "w_value": normal_values(key_of[5], (SECTIONS, KV_HEADS, GROUP * HEAD_DIM, HEAD_DIM), (GROUP * HEAD_DIM) ** -0.5, 0.1875, ((0, 128), (1, 8))),
        "batch_order": touch_ends(jax.random.randint(key_of[6], (SECTIONS,), 0, 2), jax.random.fold_in(key_of[6], 1), 0, 1).astype(jnp.int32),
        "segment_ids": jax.vmap(lambda own: jnp.searchsorted(jnp.cumsum(uneven_parts(own, 4, SEQ, SEQ // 2, 0)), jnp.arange(SEQ), side="right"))(jax.random.split(key_of[7], 2)).reshape((2, SEQ)).astype(jnp.int32),
    }


EPSILON = 1e-05

def normalize(stream, gain_row):
    widened = stream.astype(jnp.float32)
    scale_row = lax.rsqrt(lax.optimization_barrier(jnp.mean(widened * widened, axis=-1)) + EPSILON)
    normed = (widened * scale_row[:, None] * gain_row[None, :]).astype(jnp.bfloat16)
    return (widened, scale_row, normed)

def attention_parts(normed, key_weights, value_weights, segment):
    length = normed.shape[0]
    group_count = key_weights.shape[0]
    head_size = key_weights.shape[2]
    grouped = normed.reshape(length, group_count, -1).astype(jnp.float32)
    queries = normed.reshape(length, group_count, -1, head_size)
    key_rows = jnp.einsum('lke,ked->lkd', grouped, key_weights.astype(jnp.float32)).astype(jnp.bfloat16)
    value_rows = jnp.einsum('lke,ked->lkd', grouped, value_weights.astype(jnp.float32)).astype(jnp.bfloat16)
    score_scale = head_size ** (-0.5)
    scores = jnp.einsum('lkgd,mkd->kglm', queries.astype(jnp.float32), key_rows.astype(jnp.float32)) * score_scale
    position = jnp.arange(length)
    allowed = (position[None, :] <= position[:, None]) & (segment[:, None] == segment[None, :])
    scores = jnp.where(allowed[None, None], scores, -jnp.inf)
    attn_weights = jax.nn.softmax(scores, axis=-1)
    return (queries, key_rows, value_rows, attn_weights, score_scale)

def forward_layer(stream, gain_row, key_weights, value_weights, segment):
    widened, scale_row, normed = normalize(stream, gain_row)
    queries, key_rows, value_rows, attn_weights, score_scale = attention_parts(normed, key_weights, value_weights, segment)
    rounded = lax.optimization_barrier(attn_weights.astype(jnp.bfloat16))
    mixed_heads = jnp.einsum('kglm,mkd->lkgd', rounded.astype(jnp.float32), value_rows.astype(jnp.float32)).astype(jnp.bfloat16)
    return (widened + mixed_heads.reshape(stream.shape).astype(jnp.float32)).astype(jnp.bfloat16)

def backward_layer(stream, grad_rows, gain_row, key_weights, value_weights, segment):
    widened, scale_row, normed = normalize(stream, gain_row)
    queries, key_rows, value_rows, attn_weights, score_scale = attention_parts(normed, key_weights, value_weights, segment)
    rounded = lax.optimization_barrier(attn_weights.astype(jnp.bfloat16))
    length = stream.shape[0]
    group_count = key_weights.shape[0]
    out_grad = grad_rows.reshape(queries.shape).astype(jnp.float32)
    value_grad = jnp.einsum('kglm,lkgd->mkd', rounded.astype(jnp.float32), out_grad).astype(jnp.bfloat16)
    weight_grad = jnp.einsum('lkgd,mkd->kglm', out_grad, value_rows.astype(jnp.float32))
    row_terms = lax.optimization_barrier(jnp.sum(weight_grad * attn_weights, axis=-1, keepdims=True))
    score_grad = (attn_weights * (weight_grad - row_terms) * score_scale).astype(jnp.bfloat16)
    query_grad = jnp.einsum('kglm,mkd->lkgd', score_grad.astype(jnp.float32), key_rows.astype(jnp.float32))
    key_grad = jnp.einsum('kglm,lkgd->mkd', score_grad.astype(jnp.float32), queries.astype(jnp.float32)).astype(jnp.bfloat16)
    normed_grad = query_grad.reshape(length, group_count, -1)
    normed_grad = normed_grad + jnp.einsum('lkd,ked->lke', key_grad.astype(jnp.float32), key_weights.astype(jnp.float32))
    normed_grad = normed_grad + jnp.einsum('lkd,ked->lke', value_grad.astype(jnp.float32), value_weights.astype(jnp.float32))
    normed_grad = normed_grad.reshape(stream.shape)
    inner_sums = lax.optimization_barrier(jnp.sum(normed_grad * gain_row[None, :] * widened, axis=-1))
    stream_grad = scale_row[:, None] * gain_row[None, :] * normed_grad - widened * (scale_row ** 3 / D * inner_sums)[:, None]
    return (grad_rows.astype(jnp.float32) + stream_grad).astype(jnp.bfloat16)

def reference(produced, saved_inputs, upstream, norm_gain, w_key, w_value, batch_order, segment_ids):
    previous = jnp.roll(produced, 1, axis=0)
    following = jnp.roll(upstream, -1, axis=0)

    def one_section(section_items):
        prev_pair, saved_one, grad_one, gain_one, key_one, value_one, picked_batch = section_items
        forward_in = lax.dynamic_index_in_dim(prev_pair, picked_batch, 0, keepdims=False)
        segment_forward = lax.dynamic_index_in_dim(segment_ids, picked_batch, 0, keepdims=False)
        segment_backward = lax.dynamic_index_in_dim(segment_ids, 1 - picked_batch, 0, keepdims=False)
        forward_rows = forward_layer(forward_in, gain_one, key_one, value_one, segment_forward)
        backward_rows = backward_layer(saved_one, grad_one, gain_one, key_one, value_one, segment_backward)
        return (forward_rows, backward_rows)
    forward_out, input_grad = lax.map(one_section, (previous, saved_inputs, following, norm_gain, w_key, w_value, batch_order))
    return (forward_out, input_grad)
```

```python
import jax
import jax.numpy as jnp
from jax import lax
from jax.experimental import pallas as pl
from jax.experimental.pallas import tpu as pltpu
from jax.sharding import PartitionSpec as P

D = 8192
EPSILON = 1e-05
SECTIONS, TENSOR = 128, 8
SEQ, WIDTH, HEADS, HEAD = 192, 1024, 8, 128
SCALE = HEAD**-0.5
MESH = pl.DeviceIdType.MESH
F32, BF16 = jnp.float32, jnp.bfloat16
CHUNKS = ((0, 128), (128, 64))

UNITS = tuple((0, 128, (h,), 0) for h in range(HEADS)) + tuple(
    (q, 32, tuple(range(h, h + 4)), q - 96) for q in (128, 160) for h in (0, 4)
)
GROUPS = ((0, tuple(range(0, 8))), (32, (8, 9)), (64, (10, 11)))


def dot(a, b, over, precision=None):
    return lax.dot_general(a, b, ((over[:1], over[1:]), ((), ())), precision=precision, preferred_element_type=F32)


def take(ref, unit):
    q, n, heads, _ = unit
    parts = [ref[q : q + n, h * HEAD : (h + 1) * HEAD] for h in heads]
    return parts[0] if len(parts) == 1 else jnp.concatenate(parts, axis=0)


def put(ref, unit, value):
    q, n, heads, _ = unit
    for i, h in enumerate(heads):
        ref[q : q + n, h * HEAD : (h + 1) * HEAD] = value[i * n : (i + 1) * n]


def as_row(columns):
    return dot(jnp.ones((8, HEAD), F32), columns, (1, 1), lax.Precision.HIGHEST)[0:1]


def as_columns(row):
    eight = jnp.broadcast_to(row, (8, SEQ))
    return dot(eight, jnp.full((8, HEAD), 0.125, F32), (0, 0), lax.Precision.HIGHEST)


def fold(wide):
    total = wide[:, 0:HEAD]
    for h in range(1, HEADS):
        total = total + wide[:, h * HEAD : (h + 1) * HEAD]
    return total


def masks_of(segment):
    counts = [jnp.sum(jnp.where(segment < v, 1.0, 0.0), axis=1, keepdims=True) for v in (1, 2, 3)]
    start = jnp.where(segment >= 3, counts[2], jnp.where(segment >= 2, counts[1], jnp.where(segment >= 1, counts[0], 0.0)))
    key = lax.broadcasted_iota(jnp.int32, (HEAD, HEAD), 0).astype(F32)
    lane = lax.broadcasted_iota(jnp.int32, (HEAD, HEAD), 1)
    masks = {}
    query = lane.astype(F32)
    masks[0] = (key <= query) & (key >= start[:, 0:HEAD])
    tail = jnp.broadcast_to(start[:, HEAD:SEQ], (8, SEQ - HEAD)).astype(BF16)
    place = lax.broadcasted_iota(jnp.int32, (SEQ - HEAD, HEAD), 0)
    lanes = lax.broadcasted_iota(jnp.int32, (SEQ - HEAD, HEAD), 1)
    for q in (128, 160):
        pick = jnp.where(place == lax.rem(lanes, 32) + (q - 128), 1.0, 0.0).astype(BF16)
        first = dot(tail, pick, (1, 0))[0:1]
        query = (lax.rem(lane, 32) + q).astype(F32)
        keys = key + (q - 96)
        masks[q] = (keys <= query) & (keys >= first)
    return masks


def normalized(ref, out, rows, scale, gain):
    q, n = rows
    for h in range(HEADS):
        at = slice(h * HEAD, (h + 1) * HEAD)
        out[q : q + n, at] = (ref[q : q + n, at].astype(F32) * scale[q : q + n] * gain[:, at]).astype(BF16)


def weights_of(unit, normed, keys, mask):
    koff = unit[3]
    scores = dot(keys[koff : koff + HEAD, 0:HEAD], take(normed, unit), (1, 1)) * SCALE
    scores = jnp.where(mask, scores, -jnp.inf)
    grown = jnp.exp(scores - jnp.max(scores, axis=0, keepdims=True))
    return grown * (1.0 / jnp.sum(grown, axis=0, keepdims=True))


def kernel(
    order, segments, xs, gs, ys, gain_ref, wk_hbm, wv_hbm,
    fwd_out, bwd_out,
    xin, gin, y, w, nx, ny, kvx, kvy, pt, pbt, dst, dkv, dn,
    stat, cstat, xstat, xstat_in,
    load_sem, xsend, xrecv, gsend, grecv, ssend, srecv, csend, crecv, tsend, trecv,
):
    s, t = lax.axis_index("section"), lax.axis_index("tensor")
    nxt, prv = (lax.rem(s + 1, SECTIONS), t), (lax.rem(s + SECTIONS - 1, SECTIONS), t)
    peers = [(s, lax.rem(t + d, TENSOR)) for d in range(1, TENSOR)]

    barrier = pltpu.get_barrier_semaphore()
    for device in [nxt, prv] + peers:
        pl.semaphore_signal(barrier, inc=1, device_id=device, device_id_type=MESH)
    loads = [
        pltpu.make_async_copy(ys, y, load_sem.at[0]),
        pltpu.make_async_copy(wk_hbm, w.at[:, 0:HEAD], load_sem.at[1]),
        pltpu.make_async_copy(wv_hbm, w.at[:, HEAD : 2 * HEAD], load_sem.at[2]),
        pltpu.make_async_copy(xs, nx, load_sem.at[3]),
    ]
    for load in loads:
        load.start()
    gain = gain_ref[...]
    forward = order[s].astype(F32)
    segment = segments[...].astype(F32)
    seg_f = segment[0:1] + forward * (segment[1:2] - segment[0:1])
    seg_b = segment[1:2] + forward * (segment[0:1] - segment[1:2])
    loads[0].wait()
    loads[3].wait()

    def squares(ref):
        total = None
        for h in range(HEADS):
            part = ref[:, h * HEAD : (h + 1) * HEAD].astype(F32)
            total = part * part if total is None else total + part * part
        return as_row(total)

    stat[t, 0:1, :] = squares(y)
    stat[t, 1:2, :] = squares(nx)

    pl.semaphore_wait(barrier, 2 + len(peers))

    def remote(src, dst, send, recv, device):
        return pltpu.make_async_remote_copy(
            src_ref=src, dst_ref=dst, send_sem=send, recv_sem=recv, device_id=device, device_id_type=MESH
        )

    def to_peers(box, send, recv):
        return [remote(box.at[t], box.at[t], send.at[d], recv.at[t], peers[d]) for d in range(TENSOR - 1)]

    def from_peers(box, send, recv):
        for d in range(TENSOR - 1):
            slot = lax.rem(t + d + 1, TENSOR)
            remote(box.at[slot], box.at[slot], send.at[d], recv.at[slot], peers[d]).wait_recv()

    stat_sends = to_peers(stat, ssend, srecv)
    for copy in stat_sends:
        copy.start()
    g_copies = [remote(gs.at[pl.ds(q, n)], gin.at[pl.ds(q, n)], gsend.at[i], grecv.at[i], prv) for i, (q, n) in enumerate(CHUNKS)]
    x_copies = [remote(xs.at[pl.ds(q, n)], xin.at[pl.ds(q, n)], xsend.at[i], xrecv.at[i], nxt) for i, (q, n) in enumerate(CHUNKS)]
    for copy in g_copies + x_copies:
        copy.start()

    masks_b = masks_of(seg_b)
    masks_f = masks_of(seg_f)
    loads[1].wait()
    loads[2].wait()

    from_peers(stat, ssend, srecv)
    totals = jnp.sum(stat[...], axis=0)
    xstat[...] = totals[1:2]
    x_total = remote(xstat, xstat_in, tsend, trecv, nxt)
    x_total.start()

    scale_row = lax.rsqrt(totals[0:1] / D + EPSILON)
    scale = as_columns(scale_row)
    normalized(y, ny, (0, SEQ), scale, gain)
    kvy[...] = dot(ny[...], w[...], (1, 0)).astype(BF16)
    for u, unit in enumerate(UNITS):
        p = weights_of(unit, ny, kvy, masks_b[unit[0]])
        pt[:, u * HEAD : (u + 1) * HEAD] = p
        pbt[:, u * HEAD : (u + 1) * HEAD] = p.astype(BF16)

    def backward(units):
        for u in units:
            unit, at = UNITS[u], slice(u * HEAD, (u + 1) * HEAD)
            koff = unit[3]
            dp = dot(kvy[koff : koff + HEAD, HEAD : 2 * HEAD], take(gin, unit), (1, 1))
            p = pt[:, at]
            rows = jnp.sum(dp * p, axis=0, keepdims=True)
            ds = (p * (dp - rows) * SCALE).astype(BF16)
            dst[:, at] = ds
            put(dn, unit, dot(ds, kvy[koff : koff + HEAD, 0:HEAD], (0, 0)))

    def key_grads(group):
        koff, units = group
        at = slice(units[0] * HEAD, (units[-1] + 1) * HEAD)
        grads = jnp.concatenate([take(gin, UNITS[u]) for u in units], axis=0)
        queries = jnp.concatenate([take(ny, UNITS[u]) for u in units], axis=0)
        dkv[koff : koff + HEAD, 0:HEAD] += dot(dst[:, at], queries, (1, 0))
        dkv[koff : koff + HEAD, HEAD : 2 * HEAD] += dot(pbt[:, at], grads, (1, 0))

    dkv[...] = jnp.zeros_like(dkv)
    g_copies[0].wait_recv()
    backward(GROUPS[0][1])
    key_grads(GROUPS[0])
    g_copies[1].wait_recv()
    for group in GROUPS[1:]:
        backward(group[1])
        key_grads(group)
    rounded = dkv[...].astype(BF16)
    total = None
    scale_b = scale
    for h in range(HEADS):
        at = slice(h * HEAD, (h + 1) * HEAD)
        d = dn[:, at] + dot(rounded, w[at, :], (1, 1))
        scaled = d * gain[:, at]
        dn[:, at] = gin[:, at].astype(F32) + scale_b * scaled
        part = scaled * y[:, at].astype(F32)
        total = part if total is None else total + part
    cstat[t, 0:1, :] = as_row(total)
    c_sends = to_peers(cstat, csend, crecv)
    for copy in c_sends:
        copy.start()

    for copy in x_copies:
        copy.wait_recv()
    x_total.wait_recv()
    scale_f = as_columns(lax.rsqrt(xstat_in[...] / D + EPSILON))
    normalized(xin, nx, (0, SEQ), scale_f, gain)
    kvx[...] = dot(nx[...], w[...], (1, 0)).astype(BF16)
    for unit in UNITS:
        koff = unit[3]
        p = weights_of(unit, nx, kvx, masks_f[unit[0]]).astype(BF16)
        mixed = dot(p, kvx[koff : koff + HEAD, HEAD : 2 * HEAD], (0, 0)).astype(BF16).astype(F32)
        put(fwd_out, unit, (take(xin, unit).astype(F32) + mixed).astype(BF16))

    from_peers(cstat, csend, crecv)
    inner = jnp.sum(cstat[...], axis=0)
    pull = as_columns(scale_row * scale_row * scale_row / D * inner)
    for h in range(HEADS):
        at = slice(h * HEAD, (h + 1) * HEAD)
        bwd_out[:, at] = (dn[:, at] - y[:, at].astype(F32) * pull).astype(BF16)

    for copy in stat_sends + g_copies + x_copies + [x_total] + c_sends:
        copy.wait_send()


def on_device(produced, saved_inputs, upstream, norm_gain, w_key, w_value, batch_order, segment_ids):
    section = lax.axis_index("section")
    wanted = lax.dynamic_index_in_dim(batch_order, lax.rem(section + 1, SECTIONS), 0, keepdims=False)
    sent = lax.dynamic_index_in_dim(produced[0], wanted, 0, keepdims=False)
    rows = jax.ShapeDtypeStruct((SEQ, WIDTH), BF16)
    hbm, vmem = pl.BlockSpec(memory_space=pl.ANY), pl.BlockSpec(memory_space=pltpu.VMEM)
    stream = pltpu.VMEM((SEQ, WIDTH), BF16)
    wide = len(UNITS) * HEAD
    dma = pltpu.SemaphoreType.DMA
    forward_out, input_grad = pl.pallas_call(
        kernel,
        out_shape=(rows, rows),
        in_specs=[pl.BlockSpec(memory_space=pltpu.SMEM), vmem, hbm, hbm, hbm, vmem, hbm, hbm],
        out_specs=(vmem, vmem),
        scratch_shapes=[
            stream, stream, stream,
            pltpu.VMEM((WIDTH, 2 * HEAD), BF16),
            stream, stream,
            pltpu.VMEM((SEQ, 2 * HEAD), BF16), pltpu.VMEM((SEQ, 2 * HEAD), BF16),
            pltpu.VMEM((HEAD, wide), F32), pltpu.VMEM((HEAD, wide), BF16), pltpu.VMEM((HEAD, wide), BF16),
            pltpu.VMEM((SEQ, 2 * HEAD), F32), pltpu.VMEM((SEQ, WIDTH), F32),
            pltpu.VMEM((TENSOR, 2, SEQ), F32), pltpu.VMEM((TENSOR, 1, SEQ), F32),
            pltpu.VMEM((1, SEQ), F32), pltpu.VMEM((1, SEQ), F32),
            dma((4,)), dma((len(CHUNKS),)), dma((len(CHUNKS),)), dma((len(CHUNKS),)), dma((len(CHUNKS),)),
            dma((TENSOR - 1,)), dma((TENSOR,)), dma((TENSOR - 1,)), dma((TENSOR,)), dma, dma,
        ],
        compiler_params=pltpu.CompilerParams(collective_id=0, has_side_effects=True),
    )(batch_order, segment_ids, sent, upstream[0], saved_inputs[0], norm_gain, w_key[0, 0], w_value[0, 0])
    return forward_out[None], input_grad[None]


def solution(mesh):
    return jax.shard_map(
        on_device,
        mesh=mesh,
        in_specs=(
            P("section", None, None, "tensor"),
            P("section", None, "tensor"),
            P("section", None, "tensor"),
            P("section", "tensor"),
            P("section", "tensor", None, None),
            P("section", "tensor", None, None),
            P(),
            P(),
        ),
        out_specs=(P("section", None, "tensor"), P("section", None, "tensor")),
        check_vma=False,
    )
```

```python
import jax
import jax.numpy as jnp
from jax import lax
from jax.experimental import pallas as pl
from jax.experimental.pallas import tpu as pltpu
from jax.sharding import PartitionSpec as P

D = 8192
EPSILON = 1e-05
SECTIONS, TENSOR = 128, 8
SEQ, WIDTH, HEADS, HEAD = 192, 1024, 8, 128
SCALE = HEAD**-0.5
MESH = pl.DeviceIdType.MESH
F32, BF16 = jnp.float32, jnp.bfloat16
CHUNKS = ((0, 128), (128, 64))

UNITS = tuple((0, 128, (h,), 0) for h in range(HEADS)) + tuple(
    (q, 32, tuple(range(h, h + 4)), q - 96) for q in (128, 160) for h in (0, 4)
)
GROUPS = ((0, tuple(range(0, 8))), (32, (8, 9)), (64, (10, 11)))


def dot(a, b, over, precision=None):
    return lax.dot_general(a, b, ((over[:1], over[1:]), ((), ())), precision=precision, preferred_element_type=F32)


def take(ref, unit):
    q, n, heads, _ = unit
    parts = [ref[q : q + n, h * HEAD : (h + 1) * HEAD] for h in heads]
    return parts[0] if len(parts) == 1 else jnp.concatenate(parts, axis=0)


def put(ref, unit, value):
    q, n, heads, _ = unit
    for i, h in enumerate(heads):
        ref[q : q + n, h * HEAD : (h + 1) * HEAD] = value[i * n : (i + 1) * n]


def as_row(columns):
    return dot(jnp.ones((8, HEAD), F32), columns, (1, 1), lax.Precision.HIGHEST)[0:1]


def as_columns(row):
    eight = jnp.broadcast_to(row, (8, SEQ))
    return dot(eight, jnp.full((8, HEAD), 0.125, F32), (0, 0), lax.Precision.HIGHEST)


def fold(wide):
    total = wide[:, 0:HEAD]
    for h in range(1, HEADS):
        total = total + wide[:, h * HEAD : (h + 1) * HEAD]
    return total


def masks_of(segment):
    counts = [jnp.sum(jnp.where(segment < v, 1.0, 0.0), axis=1, keepdims=True) for v in (1, 2, 3)]
    start = jnp.where(segment >= 3, counts[2], jnp.where(segment >= 2, counts[1], jnp.where(segment >= 1, counts[0], 0.0)))
    key = lax.broadcasted_iota(jnp.int32, (HEAD, HEAD), 0).astype(F32)
    lane = lax.broadcasted_iota(jnp.int32, (HEAD, HEAD), 1)
    masks = {}
    query = lane.astype(F32)
    masks[0] = (key <= query) & (key >= start[:, 0:HEAD])
    tail = jnp.broadcast_to(start[:, HEAD:SEQ], (8, SEQ - HEAD)).astype(BF16)
    place = lax.broadcasted_iota(jnp.int32, (SEQ - HEAD, HEAD), 0)
    lanes = lax.broadcasted_iota(jnp.int32, (SEQ - HEAD, HEAD), 1)
    for q in (128, 160):
        pick = jnp.where(place == lax.rem(lanes, 32) + (q - 128), 1.0, 0.0).astype(BF16)
        first = dot(tail, pick, (1, 0))[0:1]
        query = (lax.rem(lane, 32) + q).astype(F32)
        keys = key + (q - 96)
        masks[q] = (keys <= query) & (keys >= first)
    return masks


def normalized(ref, out, rows, scale, gain):
    q, n = rows
    for h in range(HEADS):
        at = slice(h * HEAD, (h + 1) * HEAD)
        out[q : q + n, at] = (ref[q : q + n, at].astype(F32) * scale[q : q + n] * gain[:, at]).astype(BF16)


def weights_of(unit, normed, keys, mask):
    koff = unit[3]
    scores = dot(keys[koff : koff + HEAD, 0:HEAD], take(normed, unit), (1, 1)) * SCALE
    scores = jnp.where(mask, scores, -jnp.inf)
    grown = jnp.exp(scores - jnp.max(scores, axis=0, keepdims=True))
    return grown * (1.0 / jnp.sum(grown, axis=0, keepdims=True))


def kernel(
    order_hbm, segments_hbm, produced, gs, ys, gain_hbm, wk_hbm, wv_hbm,
    fwd_out, bwd_out,
    order, segments, gain_ref, pair, xs, xin, gin, y, w, nx, ny, kvx, kvy, pt, pbt, dst, dkv, dn,
    stat, cstat, xstat, xstat_in,
    load_sem, xsend, xrecv, gsend, grecv, ssend, srecv, csend, crecv, tsend, trecv,
    peer_in, next_in, previous_in,
):
    s, t = lax.axis_index("section"), lax.axis_index("tensor")
    nxt, prv = (lax.rem(s + 1, SECTIONS), t), (lax.rem(s + SECTIONS - 1, SECTIONS), t)
    peers = [(s, lax.rem(t + d, TENSOR)) for d in range(1, TENSOR)]
    place = lax.rem(s, 16)

    def signal(semaphore, device):
        pl.semaphore_signal(semaphore, inc=1, device_id=device, device_id_type=MESH)

    barrier = pltpu.get_barrier_semaphore()
    for d in range(TENSOR - 1):
        pl.when(t + d + 1 < TENSOR)(lambda d=d: signal(barrier, peers[d]))
    pl.when(place != 15)(lambda: signal(barrier, nxt))
    pl.when(place == 0)(lambda: signal(barrier, prv))
    loads = [
        pltpu.make_async_copy(produced, pair, load_sem.at[0]),
        pltpu.make_async_copy(order_hbm, order, load_sem.at[1]),
        pltpu.make_async_copy(ys, y, load_sem.at[2]),
        pltpu.make_async_copy(wk_hbm, w.at[:, 0:HEAD], load_sem.at[3]),
        pltpu.make_async_copy(wv_hbm, w.at[:, HEAD : 2 * HEAD], load_sem.at[4]),
        pltpu.make_async_copy(segments_hbm, segments, load_sem.at[5]),
        pltpu.make_async_copy(gain_hbm, gain_ref, load_sem.at[6]),
    ]
    for load in loads:
        load.start()
    greeted = t + jnp.where(place != 0, 1, 0) + jnp.where(place == 15, 1, 0)
    pl.when(greeted > 0)(lambda: pl.semaphore_wait(barrier, greeted))
    pl.when(place != 0)(lambda: signal(next_in, prv))
    pl.when(place == 15)(lambda: signal(previous_in, nxt))
    for d in range(TENSOR - 1):
        pl.when(t + d + 1 >= TENSOR)(lambda d=d: signal(peer_in, peers[d]))

    def remote(src, dst, send, recv, device):
        return pltpu.make_async_remote_copy(
            src_ref=src, dst_ref=dst, send_sem=send, recv_sem=recv, device_id=device, device_id_type=MESH
        )

    g_copies = [remote(gs.at[pl.ds(q, n)], gin.at[pl.ds(q, n)], gsend.at[i], grecv.at[i], prv) for i, (q, n) in enumerate(CHUNKS)]
    x_copies = [remote(xs.at[pl.ds(q, n)], xin.at[pl.ds(q, n)], xsend.at[i], xrecv.at[i], nxt) for i, (q, n) in enumerate(CHUNKS)]
    x_total = remote(xstat, xstat_in, tsend, trecv, nxt)

    @pl.when(place != 0)
    def _():
        for copy in g_copies:
            copy.start()

    loads[0].wait()
    loads[1].wait()
    wanted = order[lax.rem(s + 1, SECTIONS)]
    xs[...] = pair[wanted]

    @pl.when(place != 7)
    def _():
        pl.when(place != 15)(lambda: pl.semaphore_wait(next_in, 1))
        x_copies[0].start()

    loads[2].wait()

    def squares(ref):
        total = None
        for h in range(HEADS):
            part = ref[:, h * HEAD : (h + 1) * HEAD].astype(F32)
            total = part * part if total is None else total + part * part
        return as_row(total)

    stat[t, 0:1, :] = squares(y)
    stat[t, 1:2, :] = squares(xs)

    def to_peers(box, send, recv):
        return [remote(box.at[t], box.at[t], send.at[d], recv.at[t], peers[d]) for d in range(TENSOR - 1)]

    def from_peers(box, send, recv):
        for d in range(TENSOR - 1):
            slot = lax.rem(t + d + 1, TENSOR)
            remote(box.at[slot], box.at[slot], send.at[d], recv.at[slot], peers[d]).wait_recv()

    pl.when(t < TENSOR - 1)(lambda: pl.semaphore_wait(peer_in, TENSOR - 1 - t))
    stat_sends = to_peers(stat, ssend, srecv)
    for copy in stat_sends:
        copy.start()

    for load in loads[3:]:
        load.wait()
    gain = gain_ref[...]
    forward = order[s].astype(F32)
    segment = segments[...].astype(F32)
    masks_b = masks_of(segment[1:2] + forward * (segment[0:1] - segment[1:2]))
    masks_f = masks_of(segment[0:1] + forward * (segment[1:2] - segment[0:1]))

    from_peers(stat, ssend, srecv)
    totals = jnp.sum(stat[...], axis=0)
    xstat[...] = totals[1:2]

    @pl.when(place != 7)
    def _():
        x_total.start()
        x_copies[1].start()

    scale_row = lax.rsqrt(totals[0:1] / D + EPSILON)
    scale = as_columns(scale_row)
    normalized(y, ny, (0, SEQ), scale, gain)
    kvy[...] = dot(ny[...], w[...], (1, 0)).astype(BF16)
    for u, unit in enumerate(UNITS):
        p = weights_of(unit, ny, kvy, masks_b[unit[0]])
        pt[:, u * HEAD : (u + 1) * HEAD] = p
        pbt[:, u * HEAD : (u + 1) * HEAD] = p.astype(BF16)

    @pl.when(place == 0)
    def _():
        pl.semaphore_wait(previous_in, 1)
        for copy in g_copies:
            copy.start()

    @pl.when(place == 7)
    def _():
        pl.semaphore_wait(next_in, 1)
        for copy in (x_total, *x_copies):
            copy.start()

    def backward(units):
        for u in units:
            unit, at = UNITS[u], slice(u * HEAD, (u + 1) * HEAD)
            koff = unit[3]
            dp = dot(kvy[koff : koff + HEAD, HEAD : 2 * HEAD], take(gin, unit), (1, 1))
            p = pt[:, at]
            rows = jnp.sum(dp * p, axis=0, keepdims=True)
            ds = (p * (dp - rows) * SCALE).astype(BF16)
            dst[:, at] = ds
            put(dn, unit, dot(ds, kvy[koff : koff + HEAD, 0:HEAD], (0, 0)))

    def key_grads(group):
        koff, units = group
        at = slice(units[0] * HEAD, (units[-1] + 1) * HEAD)
        grads = jnp.concatenate([take(gin, UNITS[u]) for u in units], axis=0)
        queries = jnp.concatenate([take(ny, UNITS[u]) for u in units], axis=0)
        dkv[koff : koff + HEAD, 0:HEAD] += dot(dst[:, at], queries, (1, 0))
        dkv[koff : koff + HEAD, HEAD : 2 * HEAD] += dot(pbt[:, at], grads, (1, 0))

    dkv[...] = jnp.zeros_like(dkv)
    g_copies[0].wait_recv()
    backward(GROUPS[0][1])
    key_grads(GROUPS[0])
    g_copies[1].wait_recv()
    for group in GROUPS[1:]:
        backward(group[1])
        key_grads(group)
    rounded = dkv[...].astype(BF16)
    total = None
    for h in range(HEADS):
        at = slice(h * HEAD, (h + 1) * HEAD)
        d = dn[:, at] + dot(rounded, w[at, :], (1, 1))
        scaled = d * gain[:, at]
        dn[:, at] = gin[:, at].astype(F32) + scale * scaled
        part = scaled * y[:, at].astype(F32)
        total = part if total is None else total + part
    cstat[t, 0:1, :] = as_row(total)
    c_sends = to_peers(cstat, csend, crecv)
    for copy in c_sends:
        copy.start()

    def finish_backward():
        from_peers(cstat, csend, crecv)
        inner = jnp.sum(cstat[...], axis=0)
        pull = as_columns(scale_row * scale_row * scale_row / D * inner)
        for h in range(HEADS):
            at = slice(h * HEAD, (h + 1) * HEAD)
            bwd_out[:, at] = (dn[:, at] - y[:, at].astype(F32) * pull).astype(BF16)

    late_forward = lax.rem(s, 8) == 0
    pl.when(late_forward)(finish_backward)

    x_copies[0].wait_recv()
    x_total.wait_recv()
    scale_f = as_columns(lax.rsqrt(xstat_in[...] / D + EPSILON))
    for i, (q, n) in enumerate(CHUNKS):
        if i:
            x_copies[i].wait_recv()
        normalized(xin, nx, (q, n), scale_f, gain)
        kvx[q : q + n] = dot(nx[q : q + n], w[...], (1, 0)).astype(BF16)
        for unit in UNITS:
            if q <= unit[0] < q + n:
                koff = unit[3]
                p = weights_of(unit, nx, kvx, masks_f[unit[0]]).astype(BF16)
                mixed = dot(p, kvx[koff : koff + HEAD, HEAD : 2 * HEAD], (0, 0)).astype(BF16).astype(F32)
                put(fwd_out, unit, (take(xin, unit).astype(F32) + mixed).astype(BF16))

    pl.when(jnp.logical_not(late_forward))(finish_backward)

    for copy in stat_sends + g_copies + x_copies + [x_total] + c_sends:
        copy.wait_send()


def write_out(first, second, first_out, second_out, semaphore):
    copies = [pltpu.make_async_copy(first, first_out, semaphore.at[0]), pltpu.make_async_copy(second, second_out, semaphore.at[1])]
    for copy in copies:
        copy.start()
    for copy in copies:
        copy.wait()


def on_device(produced, saved_inputs, upstream, norm_gain, w_key, w_value, batch_order, segment_ids):
    rows = jax.ShapeDtypeStruct((SEQ, WIDTH), BF16)
    hbm, vmem = pl.BlockSpec(memory_space=pltpu.HBM), pl.BlockSpec(memory_space=pltpu.VMEM)
    stream = pltpu.VMEM((SEQ, WIDTH), BF16)
    wide = len(UNITS) * HEAD
    dma, regular = pltpu.SemaphoreType.DMA, pltpu.SemaphoreType.REGULAR
    parts = len(CHUNKS)
    forward_out, input_grad = pl.pallas_call(
        kernel,
        out_shape=(rows, rows),
        in_specs=[hbm] * 8,
        out_specs=(vmem, vmem),
        scratch_shapes=[
            pltpu.SMEM((SECTIONS,), jnp.int32), pltpu.VMEM((2, SEQ), jnp.int32), pltpu.VMEM((1, WIDTH), F32),
            pltpu.VMEM((2, SEQ, WIDTH), BF16),
            stream, stream, stream, stream,
            pltpu.VMEM((WIDTH, 2 * HEAD), BF16),
            stream, stream,
            pltpu.VMEM((SEQ, 2 * HEAD), BF16), pltpu.VMEM((SEQ, 2 * HEAD), BF16),
            pltpu.VMEM((HEAD, wide), F32), pltpu.VMEM((HEAD, wide), BF16), pltpu.VMEM((HEAD, wide), BF16),
            pltpu.VMEM((SEQ, 2 * HEAD), F32), pltpu.VMEM((SEQ, WIDTH), F32),
            pltpu.VMEM((TENSOR, 2, SEQ), F32), pltpu.VMEM((TENSOR, 1, SEQ), F32),
            pltpu.VMEM((1, SEQ), F32), pltpu.VMEM((1, SEQ), F32),
            dma((7,)), dma((parts,)), dma((parts,)), dma((parts,)), dma((parts,)),
            dma((TENSOR - 1,)), dma((TENSOR,)), dma((TENSOR - 1,)), dma((TENSOR,)), dma, dma,
            regular, regular, regular,
        ],
        compiler_params=pltpu.CompilerParams(collective_id=0, has_side_effects=True, vmem_limit_bytes=24 << 20),
    )(*[pltpu.with_memory_space_constraint(a, pltpu.HBM) for a in (batch_order, segment_ids, produced[0], upstream[0], saved_inputs[0], norm_gain, w_key[0, 0], w_value[0, 0])])
    forward_out, input_grad = pl.pallas_call(
        write_out,
        out_shape=(rows, rows),
        in_specs=[vmem, vmem],
        out_specs=(hbm, hbm),
        scratch_shapes=[dma((2,))],
        compiler_params=pltpu.CompilerParams(vmem_limit_bytes=4 << 20),
    )(forward_out, input_grad)
    return forward_out[None], input_grad[None]


def solution(mesh):
    return jax.shard_map(
        on_device,
        mesh=mesh,
        in_specs=(
            P("section", None, None, "tensor"),
            P("section", None, "tensor"),
            P("section", None, "tensor"),
            P("section", "tensor"),
            P("section", "tensor", None, None),
            P("section", "tensor", None, None),
            P(),
            P(),
        ),
        out_specs=(P("section", None, "tensor"), P("section", None, "tensor")),
        check_vma=False,
    )
```

```python
import jax
import jax.numpy as jnp
from jax import lax
from jax.experimental import pallas as pl
from jax.experimental.pallas import tpu as pltpu
from jax.sharding import PartitionSpec as P

D = 8192
EPSILON = 1e-05
SECTIONS, TENSOR = 128, 8
SEQ, WIDTH, HEADS, HEAD = 192, 1024, 8, 128
SCALE = HEAD**-0.5
MESH = pl.DeviceIdType.MESH
F32, BF16 = jnp.float32, jnp.bfloat16
CHUNKS = ((0, 128), (128, 64))
PIECES = tuple((i * 32, 32) for i in range(4)) + tuple((128 + i * 16, 16) for i in range(4))
HELD = ((0, 32), (32, 16))
X_RELAYS, G_RELAYS = (7, 6, 1), (0, 1, 6)

UNITS = tuple((0, 128, (h,), 0) for h in range(HEADS)) + tuple(
    (q, 32, tuple(range(h, h + 4)), q - 96) for q in (128, 160) for h in (0, 4)
)
GROUPS = ((0, tuple(range(0, 8))), (32, (8, 9)), (64, (10, 11)))


def dot(a, b, over, precision=None):
    return lax.dot_general(a, b, ((over[:1], over[1:]), ((), ())), precision=precision, preferred_element_type=F32)


def take(ref, unit):
    q, n, heads, _ = unit
    parts = [ref[q : q + n, h * HEAD : (h + 1) * HEAD] for h in heads]
    return parts[0] if len(parts) == 1 else jnp.concatenate(parts, axis=0)


def put(ref, unit, value):
    q, n, heads, _ = unit
    for i, h in enumerate(heads):
        ref[q : q + n, h * HEAD : (h + 1) * HEAD] = value[i * n : (i + 1) * n]


def as_row(columns):
    return dot(jnp.ones((8, HEAD), F32), columns, (1, 1), lax.Precision.HIGHEST)[0:1]


def as_columns(row):
    eight = jnp.broadcast_to(row, (8, SEQ))
    return dot(eight, jnp.full((8, HEAD), 0.125, F32), (0, 0), lax.Precision.HIGHEST)


def fold(wide):
    total = wide[:, 0:HEAD]
    for h in range(1, HEADS):
        total = total + wide[:, h * HEAD : (h + 1) * HEAD]
    return total


def masks_of(segment):
    counts = [jnp.sum(jnp.where(segment < v, 1.0, 0.0), axis=1, keepdims=True) for v in (1, 2, 3)]
    start = jnp.where(segment >= 3, counts[2], jnp.where(segment >= 2, counts[1], jnp.where(segment >= 1, counts[0], 0.0)))
    key = lax.broadcasted_iota(jnp.int32, (HEAD, HEAD), 0).astype(F32)
    lane = lax.broadcasted_iota(jnp.int32, (HEAD, HEAD), 1)
    masks = {}
    query = lane.astype(F32)
    masks[0] = (key <= query) & (key >= start[:, 0:HEAD])
    tail = jnp.broadcast_to(start[:, HEAD:SEQ], (8, SEQ - HEAD)).astype(BF16)
    place = lax.broadcasted_iota(jnp.int32, (SEQ - HEAD, HEAD), 0)
    lanes = lax.broadcasted_iota(jnp.int32, (SEQ - HEAD, HEAD), 1)
    for q in (128, 160):
        pick = jnp.where(place == lax.rem(lanes, 32) + (q - 128), 1.0, 0.0).astype(BF16)
        first = dot(tail, pick, (1, 0))[0:1]
        query = (lax.rem(lane, 32) + q).astype(F32)
        keys = key + (q - 96)
        masks[q] = (keys <= query) & (keys >= first)
    return masks


def normalized(ref, out, rows, scale, gain):
    q, n = rows
    for h in range(HEADS):
        at = slice(h * HEAD, (h + 1) * HEAD)
        out[q : q + n, at] = (ref[q : q + n, at].astype(F32) * scale[q : q + n] * gain[:, at]).astype(BF16)


def weights_of(unit, normed, keys, mask):
    koff = unit[3]
    scores = dot(keys[koff : koff + HEAD, 0:HEAD], take(normed, unit), (1, 1)) * SCALE
    scores = jnp.where(mask, scores, -jnp.inf)
    grown = jnp.exp(scores - jnp.max(scores, axis=0, keepdims=True))
    return grown * (1.0 / jnp.sum(grown, axis=0, keepdims=True))


def kernel(
    order_hbm, segments_hbm, produced, gs, ys, gain_hbm, wk_hbm, wv_hbm,
    fwd_out, bwd_out,
    order, segments, gain_ref, pair, xs, xin, gin, y, w, nx, ny, kvx, kvy, pt, pbt, dst, dkv, dn,
    stat, cstat, xstat, xstat_in,
    load_sem, xsend, xrecv, gsend, grecv, ssend, srecv, csend, crecv, tsend, trecv,
    peer_in, next_in, previous_in, x_relay_in, g_relay_in,
    x_held, g_held, x_held_recv, g_held_recv, x_held_send, g_held_send,
):
    s, t = lax.axis_index("section"), lax.axis_index("tensor")
    nxt, prv = (lax.rem(s + 1, SECTIONS), t), (lax.rem(s + SECTIONS - 1, SECTIONS), t)
    peers = [(s, lax.rem(t + d, TENSOR)) for d in range(1, TENSOR)]
    place = lax.rem(s, 16)
    x, block = lax.rem(s, 8), s // 8
    late = lax.rem(block, 2) == 1

    def partner(b):
        return b + 1 - 2 * lax.rem(b, 2)

    def relays(b, columns):
        return [(partner(b) * 8 + column, t) for column in columns]

    x_path = jnp.where(x == 7, 1, jnp.where(x == 6, 2, jnp.where(x == 1, 3, 0)))
    g_path = jnp.where(x == 0, 1, jnp.where(x == 1, 2, jnp.where(x == 6, 3, 0)))
    x_source, x_target = (partner(block) * 8 + 7, t), (lax.rem(partner(block) * 8 + 8, SECTIONS), t)
    g_source, g_target = (partner(block) * 8, t), (lax.rem(partner(block) * 8 + SECTIONS - 1, SECTIONS), t)

    def signal(semaphore, device):
        pl.semaphore_signal(semaphore, inc=1, device_id=device, device_id_type=MESH)

    barrier = pltpu.get_barrier_semaphore()
    for d in range(TENSOR - 1):
        pl.when(t + d + 1 < TENSOR)(lambda d=d: signal(barrier, peers[d]))
    pl.when(place != 15)(lambda: signal(barrier, nxt))
    pl.when(place == 0)(lambda: signal(barrier, prv))

    def greet(devices):
        for device in devices:
            signal(barrier, device)

    pl.when((x_path > 0) & jnp.logical_not(late))(lambda: greet([x_source]))
    pl.when((g_path > 0) & jnp.logical_not(late))(lambda: greet([g_source]))
    pl.when(place == 7)(lambda: greet(relays(block, X_RELAYS)))
    pl.when(place == 0)(lambda: greet(relays(block, G_RELAYS)))
    pl.when(x == 0)(lambda: greet(relays(lax.rem(s + SECTIONS - 1, SECTIONS) // 8, X_RELAYS)))
    pl.when(x == 7)(lambda: greet(relays(lax.rem(s + 1, SECTIONS) // 8, G_RELAYS)))
    loads = [
        pltpu.make_async_copy(produced, pair, load_sem.at[0]),
        pltpu.make_async_copy(order_hbm, order, load_sem.at[1]),
        pltpu.make_async_copy(ys, y, load_sem.at[2]),
        pltpu.make_async_copy(wk_hbm, w.at[:, 0:HEAD], load_sem.at[3]),
        pltpu.make_async_copy(wv_hbm, w.at[:, HEAD : 2 * HEAD], load_sem.at[4]),
        pltpu.make_async_copy(segments_hbm, segments, load_sem.at[5]),
        pltpu.make_async_copy(gain_hbm, gain_ref, load_sem.at[6]),
    ]
    for load in loads:
        load.start()
    roles = jnp.where(x_path > 0, 1, 0) + jnp.where(g_path > 0, 1, 0)
    greeted = (
        t + jnp.where(place != 0, 1, 0) + jnp.where(place == 15, 4, 0) + jnp.where(place == 8, 3, 0)
        + roles + jnp.where(late, roles, 0)
    )
    pl.when(greeted > 0)(lambda: pl.semaphore_wait(barrier, greeted))
    pl.when(place != 0)(lambda: signal(next_in, prv))
    pl.when(place == 15)(lambda: signal(previous_in, nxt))
    pl.when((x_path > 0) & late)(lambda: signal(x_relay_in, x_source))
    pl.when((g_path > 0) & late)(lambda: signal(g_relay_in, g_source))
    for d in range(TENSOR - 1):
        pl.when(t + d + 1 >= TENSOR)(lambda d=d: signal(peer_in, peers[d]))

    def remote(src, dst, send, recv, device):
        return pltpu.make_async_remote_copy(
            src_ref=src, dst_ref=dst, send_sem=send, recv_sem=recv, device_id=device, device_id_type=MESH
        )

    def straight(i, src, dst, send, recv, device):
        q, n = PIECES[i]
        return remote(src.at[pl.ds(q, n)], dst.at[pl.ds(q, n)], send.at[i], recv.at[i], device)

    def to_relay(i, src, held, send, recv, device):
        (q, n), (at, _) = PIECES[i], HELD[i // 4]
        return remote(src.at[pl.ds(q, n)], held.at[pl.ds(at, n)], send.at[i], recv.at[i // 4], device)

    def from_relay(j, path, held, dst, send, recv, device):
        at, n = HELD[j]
        rows = pl.ds(pl.multiple_of(128 * j + path * n, 16), n)
        return remote(held.at[pl.ds(at, n)], dst.at[rows], send.at[j], recv.at[4 * j + path], device)

    g_copies = [straight(i, gs, gin, gsend, grecv, prv) for i in range(8)]
    x_copies = [straight(i, xs, xin, xsend, xrecv, nxt) for i in range(8)]
    g_devices, x_devices = relays(block, G_RELAYS), relays(block, X_RELAYS)
    g_split = [g_copies[i] if i % 4 == 0 else to_relay(i, gs, g_held, gsend, g_held_recv, g_devices[i % 4 - 1]) for i in range(8)]
    x_split = [x_copies[i] if i % 4 == 0 else to_relay(i, xs, x_held, xsend, x_held_recv, x_devices[i % 4 - 1]) for i in range(8)]
    x_total = remote(xstat, xstat_in, tsend, trecv, nxt)

    def start(copies):
        for copy in copies:
            copy.start()

    pl.when((x != 0) & (place != 15))(lambda: start(g_copies))
    pl.when(place == 8)(lambda: start(g_split))

    def serve(j):
        def one(path, held, held_recv, held_send, dst, recv, target):
            @pl.when(path > 0)
            def _():
                at, n = HELD[j]
                remote(held.at[pl.ds(at, n)], held.at[pl.ds(at, n)], held_send.at[j], held_recv.at[j], target).wait_recv()
                from_relay(j, path, held, dst, held_send, recv, target).start()

        one(g_path, g_held, g_held_recv, g_held_send, gin, grecv, g_target)
        one(x_path, x_held, x_held_recv, x_held_send, xin, xrecv, x_target)

    loads[0].wait()
    loads[1].wait()
    wanted = order[lax.rem(s + 1, SECTIONS)]
    xs[...] = pair[wanted]

    pl.when(place == 15)(lambda: start(x_split[:4]))

    @pl.when(x != 7)
    def _():
        pl.semaphore_wait(next_in, 1)
        start(x_copies[:4])

    loads[2].wait()

    def squares(ref):
        total = None
        for h in range(HEADS):
            part = ref[:, h * HEAD : (h + 1) * HEAD].astype(F32)
            total = part * part if total is None else total + part * part
        return as_row(total)

    stat[t, 0:1, :] = squares(y)
    stat[t, 1:2, :] = squares(xs)

    def to_peers(box, send, recv):
        return [remote(box.at[t], box.at[t], send.at[d], recv.at[t], peers[d]) for d in range(TENSOR - 1)]

    def from_peers(box, send, recv):
        for d in range(TENSOR - 1):
            slot = lax.rem(t + d + 1, TENSOR)
            remote(box.at[slot], box.at[slot], send.at[d], recv.at[slot], peers[d]).wait_recv()

    pl.when(t < TENSOR - 1)(lambda: pl.semaphore_wait(peer_in, TENSOR - 1 - t))
    stat_sends = to_peers(stat, ssend, srecv)
    start(stat_sends)

    for load in loads[3:]:
        load.wait()
    gain = gain_ref[...]
    forward = order[s].astype(F32)
    segment = segments[...].astype(F32)
    masks_b = masks_of(segment[1:2] + forward * (segment[0:1] - segment[1:2]))
    masks_f = masks_of(segment[0:1] + forward * (segment[1:2] - segment[0:1]))

    from_peers(stat, ssend, srecv)
    totals = jnp.sum(stat[...], axis=0)
    xstat[...] = totals[1:2]

    pl.when(x != 7)(lambda: start([x_total] + x_copies[4:]))
    pl.when(place == 15)(lambda: start([x_total] + x_split[4:] + g_copies))

    scale_row = lax.rsqrt(totals[0:1] / D + EPSILON)
    scale = as_columns(scale_row)
    normalized(y, ny, (0, SEQ), scale, gain)
    kvy[...] = dot(ny[...], w[...], (1, 0)).astype(BF16)
    for u, unit in enumerate(UNITS):
        p = weights_of(unit, ny, kvy, masks_b[unit[0]])
        pt[:, u * HEAD : (u + 1) * HEAD] = p
        pbt[:, u * HEAD : (u + 1) * HEAD] = p.astype(BF16)

    @pl.when(place == 0)
    def _():
        pl.semaphore_wait(previous_in, 1)
        pl.semaphore_wait(g_relay_in, 3)
        start(g_split)

    @pl.when(place == 7)
    def _():
        pl.semaphore_wait(next_in, 1)
        pl.semaphore_wait(x_relay_in, 3)
        start([x_total] + x_split)

    def backward(units):
        for u in units:
            unit, at = UNITS[u], slice(u * HEAD, (u + 1) * HEAD)
            koff = unit[3]
            dp = dot(kvy[koff : koff + HEAD, HEAD : 2 * HEAD], take(gin, unit), (1, 1))
            p = pt[:, at]
            rows = jnp.sum(dp * p, axis=0, keepdims=True)
            ds = (p * (dp - rows) * SCALE).astype(BF16)
            dst[:, at] = ds
            put(dn, unit, dot(ds, kvy[koff : koff + HEAD, 0:HEAD], (0, 0)))

    def key_grads(group):
        koff, units = group
        at = slice(units[0] * HEAD, (units[-1] + 1) * HEAD)
        grads = jnp.concatenate([take(gin, UNITS[u]) for u in units], axis=0)
        queries = jnp.concatenate([take(ny, UNITS[u]) for u in units], axis=0)
        dkv[koff : koff + HEAD, 0:HEAD] += dot(dst[:, at], queries, (1, 0))
        dkv[koff : koff + HEAD, HEAD : 2 * HEAD] += dot(pbt[:, at], grads, (1, 0))

    dkv[...] = jnp.zeros_like(dkv)
    serve(0)
    for copy in g_copies[:4]:
        copy.wait_recv()
    backward(GROUPS[0][1])
    key_grads(GROUPS[0])
    pl.when(x == 7)(lambda: serve(1))
    for copy in g_copies[4:]:
        copy.wait_recv()
    for group in GROUPS[1:]:
        backward(group[1])
        key_grads(group)
    rounded = dkv[...].astype(BF16)
    total = None
    for h in range(HEADS):
        at = slice(h * HEAD, (h + 1) * HEAD)
        d = dn[:, at] + dot(rounded, w[at, :], (1, 1))
        scaled = d * gain[:, at]
        dn[:, at] = gin[:, at].astype(F32) + scale * scaled
        part = scaled * y[:, at].astype(F32)
        total = part if total is None else total + part
    cstat[t, 0:1, :] = as_row(total)
    c_sends = to_peers(cstat, csend, crecv)
    start(c_sends)
    pl.when(x != 7)(lambda: serve(1))

    def finish_backward():
        from_peers(cstat, csend, crecv)
        inner = jnp.sum(cstat[...], axis=0)
        pull = as_columns(scale_row * scale_row * scale_row / D * inner)
        for h in range(HEADS):
            at = slice(h * HEAD, (h + 1) * HEAD)
            bwd_out[:, at] = (dn[:, at] - y[:, at].astype(F32) * pull).astype(BF16)

    pl.when(x == 0)(finish_backward)

    for copy in x_copies[:4]:
        copy.wait_recv()
    x_total.wait_recv()
    scale_f = as_columns(lax.rsqrt(xstat_in[...] / D + EPSILON))
    for i, (q, n) in enumerate(CHUNKS):
        if i:
            for copy in x_copies[4:]:
                copy.wait_recv()
        normalized(xin, nx, (q, n), scale_f, gain)
        kvx[q : q + n] = dot(nx[q : q + n], w[...], (1, 0)).astype(BF16)
        for unit in UNITS:
            if q <= unit[0] < q + n:
                koff = unit[3]
                p = weights_of(unit, nx, kvx, masks_f[unit[0]]).astype(BF16)
                mixed = dot(p, kvx[koff : koff + HEAD, HEAD : 2 * HEAD], (0, 0)).astype(BF16).astype(F32)
                put(fwd_out, unit, (take(xin, unit).astype(F32) + mixed).astype(BF16))

    pl.when(x != 0)(finish_backward)

    for copy in stat_sends + g_copies + x_copies + [x_total] + c_sends:
        copy.wait_send()
    for path, held, held_send, dst, recv, target in (
        (g_path, g_held, g_held_send, gin, grecv, g_target),
        (x_path, x_held, x_held_send, xin, xrecv, x_target),
    ):

        @pl.when(path > 0)
        def _(path=path, held=held, held_send=held_send, dst=dst, recv=recv, target=target):
            for j in range(2):
                from_relay(j, path, held, dst, held_send, recv, target).wait_send()


def write_out(first, second, first_out, second_out, semaphore):
    copies = [pltpu.make_async_copy(first, first_out, semaphore.at[0]), pltpu.make_async_copy(second, second_out, semaphore.at[1])]
    for copy in copies:
        copy.start()
    for copy in copies:
        copy.wait()


def on_device(produced, saved_inputs, upstream, norm_gain, w_key, w_value, batch_order, segment_ids):
    rows = jax.ShapeDtypeStruct((SEQ, WIDTH), BF16)
    hbm, vmem = pl.BlockSpec(memory_space=pltpu.HBM), pl.BlockSpec(memory_space=pltpu.VMEM)
    stream = pltpu.VMEM((SEQ, WIDTH), BF16)
    wide = len(UNITS) * HEAD
    dma, regular = pltpu.SemaphoreType.DMA, pltpu.SemaphoreType.REGULAR
    parts = len(PIECES)
    held = pltpu.VMEM((48, WIDTH), BF16)
    forward_out, input_grad = pl.pallas_call(
        kernel,
        out_shape=(rows, rows),
        in_specs=[hbm] * 8,
        out_specs=(vmem, vmem),
        scratch_shapes=[
            pltpu.SMEM((SECTIONS,), jnp.int32), pltpu.VMEM((2, SEQ), jnp.int32), pltpu.VMEM((1, WIDTH), F32),
            pltpu.VMEM((2, SEQ, WIDTH), BF16),
            stream, stream, stream, stream,
            pltpu.VMEM((WIDTH, 2 * HEAD), BF16),
            stream, stream,
            pltpu.VMEM((SEQ, 2 * HEAD), BF16), pltpu.VMEM((SEQ, 2 * HEAD), BF16),
            pltpu.VMEM((HEAD, wide), F32), pltpu.VMEM((HEAD, wide), BF16), pltpu.VMEM((HEAD, wide), BF16),
            pltpu.VMEM((SEQ, 2 * HEAD), F32), pltpu.VMEM((SEQ, WIDTH), F32),
            pltpu.VMEM((TENSOR, 2, SEQ), F32), pltpu.VMEM((TENSOR, 1, SEQ), F32),
            pltpu.VMEM((1, SEQ), F32), pltpu.VMEM((1, SEQ), F32),
            dma((7,)), dma((parts,)), dma((parts,)), dma((parts,)), dma((parts,)),
            dma((TENSOR - 1,)), dma((TENSOR,)), dma((TENSOR - 1,)), dma((TENSOR,)), dma, dma,
            regular, regular, regular, regular, regular,
            held, held, dma((2,)), dma((2,)), dma((2,)), dma((2,)),
        ],
        compiler_params=pltpu.CompilerParams(collective_id=0, has_side_effects=True, vmem_limit_bytes=24 << 20),
    )(*[pltpu.with_memory_space_constraint(a, pltpu.HBM) for a in (batch_order, segment_ids, produced[0], upstream[0], saved_inputs[0], norm_gain, w_key[0, 0], w_value[0, 0])])
    forward_out, input_grad = pl.pallas_call(
        write_out,
        out_shape=(rows, rows),
        in_specs=[vmem, vmem],
        out_specs=(hbm, hbm),
        scratch_shapes=[dma((2,))],
        compiler_params=pltpu.CompilerParams(vmem_limit_bytes=4 << 20),
    )(forward_out, input_grad)
    return forward_out[None], input_grad[None]


def solution(mesh):
    return jax.shard_map(
        on_device,
        mesh=mesh,
        in_specs=(
            P("section", None, None, "tensor"),
            P("section", None, "tensor"),
            P("section", None, "tensor"),
            P("section", "tensor"),
            P("section", "tensor", None, None),
            P("section", "tensor", None, None),
            P(),
            P(),
        ),
        out_specs=(P("section", None, "tensor"), P("section", None, "tensor")),
        check_vma=False,
    )
```

```python
import jax
import jax.numpy as jnp
from jax import lax
from jax.experimental import pallas as pl
from jax.experimental.pallas import tpu as pltpu
from jax.sharding import PartitionSpec as P

D = 8192
EPSILON = 1e-05
SECTIONS, TENSOR = 128, 8
SEQ, WIDTH, HEADS, HEAD = 192, 1024, 8, 128
SCALE = HEAD**-0.5
MESH = pl.DeviceIdType.MESH
F32, BF16 = jnp.float32, jnp.bfloat16
CHUNKS = ((0, 128), (128, 64))
PIECES = tuple((i * 32, 32) for i in range(4)) + tuple((128 + i * 16, 16) for i in range(4))
HELD = ((0, 32), (32, 16))
X_RELAYS, G_RELAYS = (7, 6, 1), (0, 1, 6)

UNITS = tuple((0, 128, (h,), 0) for h in range(HEADS)) + tuple(
    (q, 32, tuple(range(h, h + 4)), q - 96) for q in (128, 160) for h in (0, 4)
)
GROUPS = ((0, tuple(range(0, 8))), (32, (8, 9)), (64, (10, 11)))


def dot(a, b, over, precision=None):
    return lax.dot_general(a, b, ((over[:1], over[1:]), ((), ())), precision=precision, preferred_element_type=F32)


def take(ref, unit):
    q, n, heads, _ = unit
    parts = [ref[q : q + n, h * HEAD : (h + 1) * HEAD] for h in heads]
    return parts[0] if len(parts) == 1 else jnp.concatenate(parts, axis=0)


def put(ref, unit, value):
    q, n, heads, _ = unit
    for i, h in enumerate(heads):
        ref[q : q + n, h * HEAD : (h + 1) * HEAD] = value[i * n : (i + 1) * n]


def as_row(columns):
    return jnp.sum(jnp.transpose(columns), axis=0, keepdims=True)


def as_columns(row):
    return jnp.transpose(jnp.broadcast_to(row, (HEAD, SEQ)))


def fold(wide):
    total = wide[:, 0:HEAD]
    for h in range(1, HEADS):
        total = total + wide[:, h * HEAD : (h + 1) * HEAD]
    return total


def masks_of(segment):
    counts = [jnp.sum(jnp.where(segment < v, 1.0, 0.0), axis=1, keepdims=True) for v in (1, 2, 3)]
    start = jnp.where(segment >= 3, counts[2], jnp.where(segment >= 2, counts[1], jnp.where(segment >= 1, counts[0], 0.0)))
    key = lax.broadcasted_iota(jnp.int32, (HEAD, HEAD), 0).astype(F32)
    lane = lax.broadcasted_iota(jnp.int32, (HEAD, HEAD), 1)
    masks = {}
    query = lane.astype(F32)
    masks[0] = (key <= query) & (key >= start[:, 0:HEAD])
    tail = jnp.broadcast_to(start[:, HEAD:SEQ], (8, SEQ - HEAD)).astype(BF16)
    place = lax.broadcasted_iota(jnp.int32, (SEQ - HEAD, HEAD), 0)
    lanes = lax.broadcasted_iota(jnp.int32, (SEQ - HEAD, HEAD), 1)
    for q in (128, 160):
        pick = jnp.where(place == lax.rem(lanes, 32) + (q - 128), 1.0, 0.0).astype(BF16)
        first = dot(tail, pick, (1, 0))[0:1]
        query = (lax.rem(lane, 32) + q).astype(F32)
        keys = key + (q - 96)
        masks[q] = (keys <= query) & (keys >= first)
    return masks


def normalized(ref, out, rows, scale, gain):
    q, n = rows
    for h in range(HEADS):
        at = slice(h * HEAD, (h + 1) * HEAD)
        out[q : q + n, at] = (ref[q : q + n, at].astype(F32) * scale[q : q + n] * gain[:, at]).astype(BF16)


def weights_of(unit, normed, keys, mask):
    koff = unit[3]
    scores = dot(keys[koff : koff + HEAD, 0:HEAD], take(normed, unit), (1, 1)) * SCALE
    scores = jnp.where(mask, scores, -jnp.inf)
    grown = jnp.exp(scores - jnp.max(scores, axis=0, keepdims=True))
    return grown * (1.0 / jnp.sum(grown, axis=0, keepdims=True))


def kernel(
    order_hbm, segments_hbm, produced, gs, ys, gain_hbm, wk_hbm, wv_hbm,
    fwd_out, bwd_out,
    order, segments, gain_ref, pair, xs, xin, gin, y, w, nx, ny, kvx, kvy, pt, pbt, dst, dkv, dn,
    stat, cstat, xstat, xstat_in,
    load_sem, xsend, xrecv, gsend, grecv, ssend, srecv, csend, crecv, tsend, trecv,
    peer_in, next_in, previous_in, x_relay_in, g_relay_in, g_target_in,
    x_held, g_held, x_held_recv, g_held_recv, x_held_send, g_held_send,
):
    s, t = lax.axis_index("section"), lax.axis_index("tensor")
    nxt, prv = (lax.rem(s + 1, SECTIONS), t), (lax.rem(s + SECTIONS - 1, SECTIONS), t)
    peers = [(s, lax.rem(t + d, TENSOR)) for d in range(1, TENSOR)]
    place = lax.rem(s, 16)
    x, block = lax.rem(s, 8), s // 8
    late = lax.rem(block, 2) == 1

    def partner(b):
        return b + 1 - 2 * lax.rem(b, 2)

    def relays(b, columns):
        return [(partner(b) * 8 + column, t) for column in columns]

    x_path = jnp.where(x == 7, 1, jnp.where(x == 6, 2, jnp.where(x == 1, 3, 0)))
    g_path = jnp.where(x == 0, 1, jnp.where(x == 1, 2, jnp.where(x == 6, 3, 0)))
    x_source, x_target = (partner(block) * 8 + 7, t), (lax.rem(partner(block) * 8 + 8, SECTIONS), t)
    g_source, g_target = (partner(block) * 8, t), (lax.rem(partner(block) * 8 + SECTIONS - 1, SECTIONS), t)

    def signal(semaphore, device):
        pl.semaphore_signal(semaphore, inc=1, device_id=device, device_id_type=MESH)

    barrier = pltpu.get_barrier_semaphore()
    for d in range(TENSOR - 1):
        pl.when(t + d + 1 < TENSOR)(lambda d=d: signal(barrier, peers[d]))
    pl.when(place != 15)(lambda: signal(barrier, nxt))
    pl.when(place == 0)(lambda: signal(barrier, prv))

    def greet(devices):
        for device in devices:
            signal(barrier, device)

    pl.when((x_path > 0) & jnp.logical_not(late))(lambda: greet([x_source]))
    pl.when((g_path > 0) & jnp.logical_not(late))(lambda: greet([g_source]))
    pl.when(place == 7)(lambda: greet(relays(block, X_RELAYS)))
    pl.when(place == 0)(lambda: greet(relays(block, G_RELAYS)))
    pl.when(x == 0)(lambda: greet(relays(lax.rem(s + SECTIONS - 1, SECTIONS) // 8, X_RELAYS)))
    pl.when(g_path > 0)(lambda: greet([g_target]))
    loads = [
        pltpu.make_async_copy(produced, pair, load_sem.at[0]),
        pltpu.make_async_copy(order_hbm, order, load_sem.at[1]),
        pltpu.make_async_copy(ys, y, load_sem.at[2]),
        pltpu.make_async_copy(wk_hbm, w.at[:, 0:HEAD], load_sem.at[3]),
        pltpu.make_async_copy(wv_hbm, w.at[:, HEAD : 2 * HEAD], load_sem.at[4]),
        pltpu.make_async_copy(segments_hbm, segments, load_sem.at[5]),
        pltpu.make_async_copy(gain_hbm, gain_ref, load_sem.at[6]),
    ]
    for load in loads:
        load.start()
    x_role, g_role = jnp.where(x_path > 0, 1, 0), jnp.where(g_path > 0, 1, 0)
    greeted = (
        t + jnp.where(place != 0, 1, 0) + jnp.where(place == 15, 4, 0) + jnp.where(place == 8, 3, 0)
        + jnp.where(x == 7, 3, 0) + x_role + jnp.where(late, x_role + g_role, 0)
    )
    pl.when(greeted > 0)(lambda: pl.semaphore_wait(barrier, greeted))
    pl.when(place != 0)(lambda: signal(next_in, prv))
    pl.when(place == 15)(lambda: signal(previous_in, nxt))

    @pl.when(x == 7)
    def _():
        for device in relays(lax.rem(s + 1, SECTIONS) // 8, G_RELAYS):
            signal(g_target_in, device)

    pl.when((x_path > 0) & late)(lambda: signal(x_relay_in, x_source))
    pl.when((g_path > 0) & late)(lambda: signal(g_relay_in, g_source))
    for d in range(TENSOR - 1):
        pl.when(t + d + 1 >= TENSOR)(lambda d=d: signal(peer_in, peers[d]))

    def remote(src, dst, send, recv, device):
        return pltpu.make_async_remote_copy(
            src_ref=src, dst_ref=dst, send_sem=send, recv_sem=recv, device_id=device, device_id_type=MESH
        )

    def straight(i, src, dst, send, recv, device):
        q, n = PIECES[i]
        return remote(src.at[pl.ds(q, n)], dst.at[pl.ds(q, n)], send.at[i], recv.at[i], device)

    def to_relay(i, src, held, send, recv, device):
        (q, n), (at, _) = PIECES[i], HELD[i // 4]
        return remote(src.at[pl.ds(q, n)], held.at[pl.ds(at, n)], send.at[i], recv.at[i // 4], device)

    def from_relay(j, path, held, dst, send, recv, device):
        at, n = HELD[j]
        rows = pl.ds(pl.multiple_of(128 * j + path * n, 16), n)
        return remote(held.at[pl.ds(at, n)], dst.at[rows], send.at[j], recv.at[4 * j + path], device)

    g_copies = [straight(i, gs, gin, gsend, grecv, prv) for i in range(8)]
    x_copies = [straight(i, xs, xin, xsend, xrecv, nxt) for i in range(8)]
    g_devices, x_devices = relays(block, G_RELAYS), relays(block, X_RELAYS)
    g_split = [g_copies[i] if i % 4 == 0 else to_relay(i, gs, g_held, gsend, g_held_recv, g_devices[i % 4 - 1]) for i in range(8)]
    x_split = [x_copies[i] if i % 4 == 0 else to_relay(i, xs, x_held, xsend, x_held_recv, x_devices[i % 4 - 1]) for i in range(8)]
    x_total = remote(xstat, xstat_in, tsend, trecv, nxt)

    def start(copies):
        for copy in copies:
            copy.start()

    pl.when((x != 0) & (place != 15))(lambda: start(g_copies))
    pl.when(place == 8)(lambda: start(g_split))

    def serve(j):
        def one(path, held, held_recv, held_send, dst, recv, target):
            @pl.when(path > 0)
            def _():
                at, n = HELD[j]
                remote(held.at[pl.ds(at, n)], held.at[pl.ds(at, n)], held_send.at[j], held_recv.at[j], target).wait_recv()
                from_relay(j, path, held, dst, held_send, recv, target).start()

        one(g_path, g_held, g_held_recv, g_held_send, gin, grecv, g_target)
        one(x_path, x_held, x_held_recv, x_held_send, xin, xrecv, x_target)

    loads[0].wait()
    loads[1].wait()
    wanted = order[lax.rem(s + 1, SECTIONS)]
    xs[...] = pair[wanted]

    pl.when(place == 15)(lambda: start(x_split + g_copies))

    @pl.when(x != 7)
    def _():
        pl.semaphore_wait(next_in, 1)
        start(x_copies[:4])

    loads[2].wait()

    def squares(ref):
        total = None
        for h in range(HEADS):
            part = ref[:, h * HEAD : (h + 1) * HEAD].astype(F32)
            total = part * part if total is None else total + part * part
        return as_row(total)

    stat[t, 0:1, :] = squares(y)
    stat[t, 1:2, :] = squares(xs)

    def to_peers(box, send, recv):
        return [remote(box.at[t], box.at[t], send.at[d], recv.at[t], peers[d]) for d in range(TENSOR - 1)]

    def from_peers(box, send, recv):
        for d in range(TENSOR - 1):
            slot = lax.rem(t + d + 1, TENSOR)
            remote(box.at[slot], box.at[slot], send.at[d], recv.at[slot], peers[d]).wait_recv()

    pl.when(t < TENSOR - 1)(lambda: pl.semaphore_wait(peer_in, TENSOR - 1 - t))
    stat_sends = to_peers(stat, ssend, srecv)
    start(stat_sends)

    for load in loads[3:]:
        load.wait()
    gain = gain_ref[...]
    forward = order[s].astype(F32)
    segment = segments[...].astype(F32)
    masks_b = masks_of(segment[1:2] + forward * (segment[0:1] - segment[1:2]))
    masks_f = masks_of(segment[0:1] + forward * (segment[1:2] - segment[0:1]))

    from_peers(stat, ssend, srecv)
    totals = jnp.sum(stat[...], axis=0)
    xstat[...] = totals[1:2]

    pl.when(x != 7)(lambda: start([x_total] + x_copies[4:]))
    pl.when(place == 15)(lambda: start([x_total]))

    scale_row = lax.rsqrt(totals[0:1] / D + EPSILON)
    scale = as_columns(scale_row)
    normalized(y, ny, (0, SEQ), scale, gain)
    kvy[...] = dot(ny[...], w[...], (1, 0)).astype(BF16)
    for u, unit in enumerate(UNITS):
        p = weights_of(unit, ny, kvy, masks_b[unit[0]])
        pt[:, u * HEAD : (u + 1) * HEAD] = p
        pbt[:, u * HEAD : (u + 1) * HEAD] = p.astype(BF16)

    @pl.when(place == 0)
    def _():
        pl.semaphore_wait(previous_in, 1)
        pl.semaphore_wait(g_relay_in, 3)
        start(g_split)

    @pl.when(place == 7)
    def _():
        pl.semaphore_wait(next_in, 1)
        pl.semaphore_wait(x_relay_in, 3)
        start([x_total] + x_split)

    def backward(units):
        for u in units:
            unit, at = UNITS[u], slice(u * HEAD, (u + 1) * HEAD)
            koff = unit[3]
            dp = dot(kvy[koff : koff + HEAD, HEAD : 2 * HEAD], take(gin, unit), (1, 1))
            p = pt[:, at]
            rows = jnp.sum(dp * p, axis=0, keepdims=True)
            ds = (p * (dp - rows) * SCALE).astype(BF16)
            dst[:, at] = ds
            put(dn, unit, dot(ds, kvy[koff : koff + HEAD, 0:HEAD], (0, 0)))

    def key_grads(group):
        koff, units = group
        at = slice(units[0] * HEAD, (units[-1] + 1) * HEAD)
        grads = jnp.concatenate([take(gin, UNITS[u]) for u in units], axis=0)
        queries = jnp.concatenate([take(ny, UNITS[u]) for u in units], axis=0)
        dkv[koff : koff + HEAD, 0:HEAD] += dot(dst[:, at], queries, (1, 0))
        dkv[koff : koff + HEAD, HEAD : 2 * HEAD] += dot(pbt[:, at], grads, (1, 0))

    dkv[...] = jnp.zeros_like(dkv)
    pl.when(g_path > 0)(lambda: pl.semaphore_wait(g_target_in, 1))
    serve(0)
    for copy in g_copies[:4]:
        copy.wait_recv()
    backward(GROUPS[0][1])
    key_grads(GROUPS[0])
    serve(1)
    for copy in g_copies[4:]:
        copy.wait_recv()
    for group in GROUPS[1:]:
        backward(group[1])
        key_grads(group)
    rounded = dkv[...].astype(BF16)
    total = None
    for h in range(HEADS):
        at = slice(h * HEAD, (h + 1) * HEAD)
        d = dn[:, at] + dot(rounded, w[at, :], (1, 1))
        scaled = d * gain[:, at]
        dn[:, at] = gin[:, at].astype(F32) + scale * scaled
        part = scaled * y[:, at].astype(F32)
        total = part if total is None else total + part
    cstat[t, 0:1, :] = as_row(total)
    c_sends = to_peers(cstat, csend, crecv)
    start(c_sends)

    def finish_backward():
        from_peers(cstat, csend, crecv)
        inner = jnp.sum(cstat[...], axis=0)
        pull = as_columns(scale_row * scale_row * scale_row / D * inner)
        for h in range(HEADS):
            at = slice(h * HEAD, (h + 1) * HEAD)
            bwd_out[:, at] = (dn[:, at] - y[:, at].astype(F32) * pull).astype(BF16)

    pl.when(x == 0)(finish_backward)

    for copy in x_copies[:4]:
        copy.wait_recv()
    x_total.wait_recv()
    scale_f = as_columns(lax.rsqrt(xstat_in[...] / D + EPSILON))
    for i, (q, n) in enumerate(CHUNKS):
        if i:
            for copy in x_copies[4:]:
                copy.wait_recv()
        normalized(xin, nx, (q, n), scale_f, gain)
        kvx[q : q + n] = dot(nx[q : q + n], w[...], (1, 0)).astype(BF16)
        for unit in UNITS:
            if q <= unit[0] < q + n:
                koff = unit[3]
                p = weights_of(unit, nx, kvx, masks_f[unit[0]]).astype(BF16)
                mixed = dot(p, kvx[koff : koff + HEAD, HEAD : 2 * HEAD], (0, 0)).astype(BF16).astype(F32)
                put(fwd_out, unit, (take(xin, unit).astype(F32) + mixed).astype(BF16))

    pl.when(x != 0)(finish_backward)

    for copy in stat_sends + g_copies + x_copies + [x_total] + c_sends:
        copy.wait_send()
    for path, held, held_send, dst, recv, target in (
        (g_path, g_held, g_held_send, gin, grecv, g_target),
        (x_path, x_held, x_held_send, xin, xrecv, x_target),
    ):

        @pl.when(path > 0)
        def _(path=path, held=held, held_send=held_send, dst=dst, recv=recv, target=target):
            for j in range(2):
                from_relay(j, path, held, dst, held_send, recv, target).wait_send()


def write_out(first, second, first_out, second_out, semaphore):
    copies = [pltpu.make_async_copy(first, first_out, semaphore.at[0]), pltpu.make_async_copy(second, second_out, semaphore.at[1])]
    for copy in copies:
        copy.start()
    for copy in copies:
        copy.wait()


def on_device(produced, saved_inputs, upstream, norm_gain, w_key, w_value, batch_order, segment_ids):
    rows = jax.ShapeDtypeStruct((SEQ, WIDTH), BF16)
    hbm, vmem = pl.BlockSpec(memory_space=pltpu.HBM), pl.BlockSpec(memory_space=pltpu.VMEM)
    stream = pltpu.VMEM((SEQ, WIDTH), BF16)
    wide = len(UNITS) * HEAD
    dma, regular = pltpu.SemaphoreType.DMA, pltpu.SemaphoreType.REGULAR
    parts = len(PIECES)
    held = pltpu.VMEM((48, WIDTH), BF16)
    forward_out, input_grad = pl.pallas_call(
        kernel,
        out_shape=(rows, rows),
        in_specs=[hbm] * 8,
        out_specs=(vmem, vmem),
        scratch_shapes=[
            pltpu.SMEM((SECTIONS,), jnp.int32), pltpu.VMEM((2, SEQ), jnp.int32), pltpu.VMEM((1, WIDTH), F32),
            pltpu.VMEM((2, SEQ, WIDTH), BF16),
            stream, stream, stream, stream,
            pltpu.VMEM((WIDTH, 2 * HEAD), BF16),
            stream, stream,
            pltpu.VMEM((SEQ, 2 * HEAD), BF16), pltpu.VMEM((SEQ, 2 * HEAD), BF16),
            pltpu.VMEM((HEAD, wide), F32), pltpu.VMEM((HEAD, wide), BF16), pltpu.VMEM((HEAD, wide), BF16),
            pltpu.VMEM((SEQ, 2 * HEAD), F32), pltpu.VMEM((SEQ, WIDTH), F32),
            pltpu.VMEM((TENSOR, 2, SEQ), F32), pltpu.VMEM((TENSOR, 1, SEQ), F32),
            pltpu.VMEM((1, SEQ), F32), pltpu.VMEM((1, SEQ), F32),
            dma((7,)), dma((parts,)), dma((parts,)), dma((parts,)), dma((parts,)),
            dma((TENSOR - 1,)), dma((TENSOR,)), dma((TENSOR - 1,)), dma((TENSOR,)), dma, dma,
            regular, regular, regular, regular, regular, regular,
            held, held, dma((2,)), dma((2,)), dma((2,)), dma((2,)),
        ],
        compiler_params=pltpu.CompilerParams(collective_id=0, has_side_effects=True, vmem_limit_bytes=24 << 20),
    )(*[pltpu.with_memory_space_constraint(a, pltpu.HBM) for a in (batch_order, segment_ids, produced[0], upstream[0], saved_inputs[0], norm_gain, w_key[0, 0], w_value[0, 0])])
    forward_out, input_grad = pl.pallas_call(
        write_out,
        out_shape=(rows, rows),
        in_specs=[vmem, vmem],
        out_specs=(hbm, hbm),
        scratch_shapes=[dma((2,))],
        compiler_params=pltpu.CompilerParams(vmem_limit_bytes=4 << 20),
    )(forward_out, input_grad)
    return forward_out[None], input_grad[None]


def solution(mesh):
    return jax.shard_map(
        on_device,
        mesh=mesh,
        in_specs=(
            P("section", None, None, "tensor"),
            P("section", None, "tensor"),
            P("section", None, "tensor"),
            P("section", "tensor"),
            P("section", "tensor", None, None),
            P("section", "tensor", None, None),
            P(),
            P(),
        ),
        out_specs=(P("section", None, "tensor"), P("section", None, "tensor")),
        check_vma=False,
    )
```

```python
import jax
import jax.numpy as jnp
from jax import lax
from jax.experimental import pallas as pl
from jax.experimental.pallas import tpu as pltpu
from jax.sharding import PartitionSpec as P

D = 8192
EPSILON = 1e-05
SECTIONS, TENSOR = 128, 8
SEQ, WIDTH, HEADS, HEAD = 192, 1024, 8, 128
SCALE = HEAD**-0.5
MESH = pl.DeviceIdType.MESH
F32, BF16 = jnp.float32, jnp.bfloat16
CHUNKS = ((0, 128), (128, 64))
PIECES = tuple((i * 32, 32) for i in range(4)) + tuple((128 + i * 16, 16) for i in range(4))
HELD = ((0, 32), (32, 16))
X_RELAYS, G_RELAYS = (7, 6, 1), (0, 1, 6)

UNITS = tuple((0, 128, (h,), 0) for h in range(HEADS)) + tuple(
    (q, 32, tuple(range(h, h + 4)), q - 96) for q in (128, 160) for h in (0, 4)
)
GROUPS = ((0, tuple(range(0, 8))), (32, (8, 9)), (64, (10, 11)))


def dot(a, b, over, precision=None):
    return lax.dot_general(a, b, ((over[:1], over[1:]), ((), ())), precision=precision, preferred_element_type=F32)


def take(ref, unit):
    q, n, heads, _ = unit
    parts = [ref[q : q + n, h * HEAD : (h + 1) * HEAD] for h in heads]
    return parts[0] if len(parts) == 1 else jnp.concatenate(parts, axis=0)


def put(ref, unit, value):
    q, n, heads, _ = unit
    for i, h in enumerate(heads):
        ref[q : q + n, h * HEAD : (h + 1) * HEAD] = value[i * n : (i + 1) * n]


def as_row(columns):
    return jnp.sum(jnp.transpose(columns), axis=0, keepdims=True)


def as_columns(row):
    return jnp.transpose(jnp.broadcast_to(row, (HEAD, SEQ)))


def fold(wide):
    total = wide[:, 0:HEAD]
    for h in range(1, HEADS):
        total = total + wide[:, h * HEAD : (h + 1) * HEAD]
    return total


def masks_of(segment):
    counts = [jnp.sum(jnp.where(segment < v, 1.0, 0.0), axis=1, keepdims=True) for v in (1, 2, 3)]
    start = jnp.where(segment >= 3, counts[2], jnp.where(segment >= 2, counts[1], jnp.where(segment >= 1, counts[0], 0.0)))
    key = lax.broadcasted_iota(jnp.int32, (HEAD, HEAD), 0).astype(F32)
    lane = lax.broadcasted_iota(jnp.int32, (HEAD, HEAD), 1)
    masks = {}
    query = lane.astype(F32)
    masks[0] = (key <= query) & (key >= start[:, 0:HEAD])
    tail = jnp.broadcast_to(start[:, HEAD:SEQ], (8, SEQ - HEAD)).astype(BF16)
    place = lax.broadcasted_iota(jnp.int32, (SEQ - HEAD, HEAD), 0)
    lanes = lax.broadcasted_iota(jnp.int32, (SEQ - HEAD, HEAD), 1)
    for q in (128, 160):
        pick = jnp.where(place == lax.rem(lanes, 32) + (q - 128), 1.0, 0.0).astype(BF16)
        first = dot(tail, pick, (1, 0))[0:1]
        query = (lax.rem(lane, 32) + q).astype(F32)
        keys = key + (q - 96)
        masks[q] = (keys <= query) & (keys >= first)
    return masks


def normalized(ref, out, rows, scale, gain):
    q, n = rows
    for h in range(HEADS):
        at = slice(h * HEAD, (h + 1) * HEAD)
        out[q : q + n, at] = (ref[q : q + n, at].astype(F32) * scale[q : q + n] * gain[:, at]).astype(BF16)


def weights_of(unit, normed, keys, mask):
    koff = unit[3]
    scores = dot(keys[koff : koff + HEAD, 0:HEAD], take(normed, unit), (1, 1)) * SCALE
    scores = jnp.where(mask, scores, -jnp.inf)
    grown = jnp.exp(scores - jnp.max(scores, axis=0, keepdims=True))
    return grown * (1.0 / jnp.sum(grown, axis=0, keepdims=True))


def kernel(
    order_hbm, segments_hbm, produced, gs, ys, gain_hbm, wk_hbm, wv_hbm,
    fwd_out, bwd_out,
    order, segments, gain_ref, pair, xs, xin, gin, y, w, nx, ny, kvx, kvy, pt, pbt, dst, dkv, dn,
    stat, cstat, xstat, xstat_in,
    load_sem, xsend, xrecv, gsend, grecv, ssend, srecv, csend, crecv, tsend, trecv,
    peer_in, next_in, previous_in, x_relay_in, g_relay_in, g_target_in,
    x_held, g_held, x_held_recv, g_held_recv, x_held_send, g_held_send,
):
    s, t = lax.axis_index("section"), lax.axis_index("tensor")
    nxt, prv = (lax.rem(s + 1, SECTIONS), t), (lax.rem(s + SECTIONS - 1, SECTIONS), t)
    peers = [(s, lax.rem(t + d, TENSOR)) for d in range(1, TENSOR)]
    place = lax.rem(s, 16)
    x, block = lax.rem(s, 8), s // 8
    late = lax.rem(block, 2) == 1

    def partner(b):
        return b + 1 - 2 * lax.rem(b, 2)

    def relays(b, columns):
        return [(partner(b) * 8 + column, t) for column in columns]

    x_path = jnp.where(x == 7, 1, jnp.where(x == 6, 2, jnp.where(x == 1, 3, 0)))
    g_path = jnp.where(x == 0, 1, jnp.where(x == 1, 2, jnp.where(x == 6, 3, 0)))
    x_source, x_target = (partner(block) * 8 + 7, t), (lax.rem(partner(block) * 8 + 8, SECTIONS), t)
    g_source, g_target = (partner(block) * 8, t), (lax.rem(partner(block) * 8 + SECTIONS - 1, SECTIONS), t)

    def signal(semaphore, device):
        pl.semaphore_signal(semaphore, inc=1, device_id=device, device_id_type=MESH)

    barrier = pltpu.get_barrier_semaphore()
    for d in range(TENSOR - 1):
        pl.when(t + d + 1 < TENSOR)(lambda d=d: signal(barrier, peers[d]))
    pl.when(place != 15)(lambda: signal(barrier, nxt))
    pl.when(place == 0)(lambda: signal(barrier, prv))

    def greet(devices):
        for device in devices:
            signal(barrier, device)

    pl.when((x_path > 0) & jnp.logical_not(late))(lambda: greet([x_source]))
    pl.when((g_path > 0) & jnp.logical_not(late))(lambda: greet([g_source]))
    pl.when(place == 7)(lambda: greet(relays(block, X_RELAYS)))
    pl.when(place == 0)(lambda: greet(relays(block, G_RELAYS)))
    pl.when(x == 0)(lambda: greet(relays(lax.rem(s + SECTIONS - 1, SECTIONS) // 8, X_RELAYS)))
    pl.when(g_path > 0)(lambda: greet([g_target]))
    loads = [
        pltpu.make_async_copy(produced, pair, load_sem.at[0]),
        pltpu.make_async_copy(order_hbm, order, load_sem.at[1]),
        pltpu.make_async_copy(ys, y, load_sem.at[2]),
        pltpu.make_async_copy(wk_hbm, w.at[:, 0:HEAD], load_sem.at[3]),
        pltpu.make_async_copy(wv_hbm, w.at[:, HEAD : 2 * HEAD], load_sem.at[4]),
        pltpu.make_async_copy(segments_hbm, segments, load_sem.at[5]),
        pltpu.make_async_copy(gain_hbm, gain_ref, load_sem.at[6]),
    ]
    for load in loads:
        load.start()
    x_role, g_role = jnp.where(x_path > 0, 1, 0), jnp.where(g_path > 0, 1, 0)
    greeted = (
        t + jnp.where(place != 0, 1, 0) + jnp.where(place == 15, 4, 0) + jnp.where(place == 8, 3, 0)
        + jnp.where(x == 7, 3, 0) + x_role + jnp.where(late, x_role + g_role, 0)
    )
    pl.when(greeted > 0)(lambda: pl.semaphore_wait(barrier, greeted))
    pl.when(place != 0)(lambda: signal(next_in, prv))
    pl.when(place == 15)(lambda: signal(previous_in, nxt))

    @pl.when(x == 7)
    def _():
        for device in relays(lax.rem(s + 1, SECTIONS) // 8, G_RELAYS):
            signal(g_target_in, device)

    pl.when((x_path > 0) & late)(lambda: signal(x_relay_in, x_source))
    pl.when((g_path > 0) & late)(lambda: signal(g_relay_in, g_source))
    for d in range(TENSOR - 1):
        pl.when(t + d + 1 >= TENSOR)(lambda d=d: signal(peer_in, peers[d]))

    def remote(src, dst, send, recv, device):
        return pltpu.make_async_remote_copy(
            src_ref=src, dst_ref=dst, send_sem=send, recv_sem=recv, device_id=device, device_id_type=MESH
        )

    def straight(i, src, dst, send, recv, device):
        q, n = PIECES[i]
        return remote(src.at[pl.ds(q, n)], dst.at[pl.ds(q, n)], send.at[i], recv.at[i], device)

    def to_relay(i, src, held, send, recv, device):
        (q, n), (at, _) = PIECES[i], HELD[i // 4]
        return remote(src.at[pl.ds(q, n)], held.at[pl.ds(at, n)], send.at[i], recv.at[i // 4], device)

    def from_relay(j, path, held, dst, send, recv, device):
        at, n = HELD[j]
        rows = pl.ds(pl.multiple_of(128 * j + path * n, 16), n)
        return remote(held.at[pl.ds(at, n)], dst.at[rows], send.at[j], recv.at[4 * j + path], device)

    g_copies = [straight(i, gs, gin, gsend, grecv, prv) for i in range(8)]
    x_copies = [straight(i, xs, xin, xsend, xrecv, nxt) for i in range(8)]
    g_devices, x_devices = relays(block, G_RELAYS), relays(block, X_RELAYS)
    g_split = [g_copies[i] if i % 4 == 0 else to_relay(i, gs, g_held, gsend, g_held_recv, g_devices[i % 4 - 1]) for i in range(8)]
    x_split = [x_copies[i] if i % 4 == 0 else to_relay(i, xs, x_held, xsend, x_held_recv, x_devices[i % 4 - 1]) for i in range(8)]
    x_total = remote(xstat, xstat_in, tsend, trecv, nxt)

    def start(copies):
        for copy in copies:
            copy.start()

    pl.when((x != 0) & (place != 15))(lambda: start(g_copies))
    pl.when(place == 8)(lambda: start(g_split))

    def serve(j, path, held, held_recv, held_send, dst, recv, target):
        at, n = HELD[j]
        remote(held.at[pl.ds(at, n)], held.at[pl.ds(at, n)], held_send.at[j], held_recv.at[j], target).wait_recv()
        from_relay(j, path, held, dst, held_send, recv, target).start()

    def serve_g():
        pl.semaphore_wait(g_target_in, 1)
        for j in range(2):
            serve(j, g_path, g_held, g_held_recv, g_held_send, gin, grecv, g_target)

    def serve_x(j):
        serve(j, x_path, x_held, x_held_recv, x_held_send, xin, xrecv, x_target)

    own_first = (place == 0) & (s != 0)

    loads[0].wait()
    loads[1].wait()
    wanted = order[lax.rem(s + 1, SECTIONS)]
    xs[...] = pair[wanted]

    pl.when(place == 15)(lambda: start(x_split + g_copies))

    @pl.when(x != 7)
    def _():
        pl.semaphore_wait(next_in, 1)
        start(x_copies[:4])

    loads[2].wait()

    def squares(ref):
        total = None
        for h in range(HEADS):
            part = ref[:, h * HEAD : (h + 1) * HEAD].astype(F32)
            total = part * part if total is None else total + part * part
        return as_row(total)

    stat[t, 0:1, :] = squares(y)
    stat[t, 1:2, :] = squares(xs)

    def to_peers(box, send, recv):
        return [remote(box.at[t], box.at[t], send.at[d], recv.at[t], peers[d]) for d in range(TENSOR - 1)]

    def from_peers(box, send, recv):
        for d in range(TENSOR - 1):
            slot = lax.rem(t + d + 1, TENSOR)
            remote(box.at[slot], box.at[slot], send.at[d], recv.at[slot], peers[d]).wait_recv()

    pl.when(t < TENSOR - 1)(lambda: pl.semaphore_wait(peer_in, TENSOR - 1 - t))
    stat_sends = to_peers(stat, ssend, srecv)
    start(stat_sends)

    for load in loads[3:]:
        load.wait()
    gain = gain_ref[...]
    forward = order[s].astype(F32)
    segment = segments[...].astype(F32)
    masks_b = masks_of(segment[1:2] + forward * (segment[0:1] - segment[1:2]))
    masks_f = masks_of(segment[0:1] + forward * (segment[1:2] - segment[0:1]))

    from_peers(stat, ssend, srecv)
    totals = jnp.sum(stat[...], axis=0)
    xstat[...] = totals[1:2]

    pl.when(x != 7)(lambda: start([x_total] + x_copies[4:]))
    pl.when(place == 15)(lambda: start([x_total]))

    scale_row = lax.rsqrt(totals[0:1] / D + EPSILON)
    scale = as_columns(scale_row)
    normalized(y, ny, (0, SEQ), scale, gain)
    kvy[...] = dot(ny[...], w[...], (1, 0)).astype(BF16)
    for u, unit in enumerate(UNITS):
        p = weights_of(unit, ny, kvy, masks_b[unit[0]])
        pt[:, u * HEAD : (u + 1) * HEAD] = p
        pbt[:, u * HEAD : (u + 1) * HEAD] = p.astype(BF16)

    @pl.when(place == 0)
    def _():
        pl.semaphore_wait(previous_in, 1)
        pl.semaphore_wait(g_relay_in, 3)
        start(g_split)

    @pl.when(place == 7)
    def _():
        pl.semaphore_wait(next_in, 1)
        pl.semaphore_wait(x_relay_in, 3)
        start([x_total] + x_split)

    def backward(units):
        for u in units:
            unit, at = UNITS[u], slice(u * HEAD, (u + 1) * HEAD)
            koff = unit[3]
            dp = dot(kvy[koff : koff + HEAD, HEAD : 2 * HEAD], take(gin, unit), (1, 1))
            p = pt[:, at]
            rows = jnp.sum(dp * p, axis=0, keepdims=True)
            ds = (p * (dp - rows) * SCALE).astype(BF16)
            dst[:, at] = ds
            put(dn, unit, dot(ds, kvy[koff : koff + HEAD, 0:HEAD], (0, 0)))

    def key_grads(group):
        koff, units = group
        at = slice(units[0] * HEAD, (units[-1] + 1) * HEAD)
        grads = jnp.concatenate([take(gin, UNITS[u]) for u in units], axis=0)
        queries = jnp.concatenate([take(ny, UNITS[u]) for u in units], axis=0)
        dkv[koff : koff + HEAD, 0:HEAD] += dot(dst[:, at], queries, (1, 0))
        dkv[koff : koff + HEAD, HEAD : 2 * HEAD] += dot(pbt[:, at], grads, (1, 0))

    dkv[...] = jnp.zeros_like(dkv)
    pl.when((g_path > 0) & jnp.logical_not(own_first))(serve_g)
    pl.when(x == 7)(lambda: serve_x(0))
    for copy in g_copies[:4]:
        copy.wait_recv()
    backward(GROUPS[0][1])
    key_grads(GROUPS[0])
    pl.when((x_path > 0) & (x != 7))(lambda: serve_x(0))
    pl.when(x_path > 0)(lambda: serve_x(1))
    for copy in g_copies[4:]:
        copy.wait_recv()
    for group in GROUPS[1:]:
        backward(group[1])
        key_grads(group)
    rounded = dkv[...].astype(BF16)
    total = None
    for h in range(HEADS):
        at = slice(h * HEAD, (h + 1) * HEAD)
        d = dn[:, at] + dot(rounded, w[at, :], (1, 1))
        scaled = d * gain[:, at]
        dn[:, at] = gin[:, at].astype(F32) + scale * scaled
        part = scaled * y[:, at].astype(F32)
        total = part if total is None else total + part
    cstat[t, 0:1, :] = as_row(total)
    c_sends = to_peers(cstat, csend, crecv)
    start(c_sends)
    pl.when(own_first)(serve_g)

    def finish_backward():
        from_peers(cstat, csend, crecv)
        inner = jnp.sum(cstat[...], axis=0)
        pull = as_columns(scale_row * scale_row * scale_row / D * inner)
        for h in range(HEADS):
            at = slice(h * HEAD, (h + 1) * HEAD)
            bwd_out[:, at] = (dn[:, at] - y[:, at].astype(F32) * pull).astype(BF16)

    finish_first = (x == 0) & (s != 0)
    pl.when(finish_first)(finish_backward)

    for copy in x_copies[:4]:
        copy.wait_recv()
    x_total.wait_recv()
    scale_f = as_columns(lax.rsqrt(xstat_in[...] / D + EPSILON))
    for i, (q, n) in enumerate(CHUNKS):
        if i:
            for copy in x_copies[4:]:
                copy.wait_recv()
        normalized(xin, nx, (q, n), scale_f, gain)
        kvx[q : q + n] = dot(nx[q : q + n], w[...], (1, 0)).astype(BF16)
        for unit in UNITS:
            if q <= unit[0] < q + n:
                koff = unit[3]
                p = weights_of(unit, nx, kvx, masks_f[unit[0]]).astype(BF16)
                mixed = dot(p, kvx[koff : koff + HEAD, HEAD : 2 * HEAD], (0, 0)).astype(BF16).astype(F32)
                put(fwd_out, unit, (take(xin, unit).astype(F32) + mixed).astype(BF16))

    pl.when(jnp.logical_not(finish_first))(finish_backward)

    for copy in stat_sends + g_copies + x_copies + [x_total] + c_sends:
        copy.wait_send()
    for path, held, held_send, dst, recv, target in (
        (g_path, g_held, g_held_send, gin, grecv, g_target),
        (x_path, x_held, x_held_send, xin, xrecv, x_target),
    ):

        @pl.when(path > 0)
        def _(path=path, held=held, held_send=held_send, dst=dst, recv=recv, target=target):
            for j in range(2):
                from_relay(j, path, held, dst, held_send, recv, target).wait_send()


def write_out(first, second, first_out, second_out, semaphore):
    copies = [pltpu.make_async_copy(first, first_out, semaphore.at[0]), pltpu.make_async_copy(second, second_out, semaphore.at[1])]
    for copy in copies:
        copy.start()
    for copy in copies:
        copy.wait()


def on_device(produced, saved_inputs, upstream, norm_gain, w_key, w_value, batch_order, segment_ids):
    rows = jax.ShapeDtypeStruct((SEQ, WIDTH), BF16)
    hbm, vmem = pl.BlockSpec(memory_space=pltpu.HBM), pl.BlockSpec(memory_space=pltpu.VMEM)
    stream = pltpu.VMEM((SEQ, WIDTH), BF16)
    wide = len(UNITS) * HEAD
    dma, regular = pltpu.SemaphoreType.DMA, pltpu.SemaphoreType.REGULAR
    parts = len(PIECES)
    held = pltpu.VMEM((48, WIDTH), BF16)
    forward_out, input_grad = pl.pallas_call(
        kernel,
        out_shape=(rows, rows),
        in_specs=[hbm] * 8,
        out_specs=(vmem, vmem),
        scratch_shapes=[
            pltpu.SMEM((SECTIONS,), jnp.int32), pltpu.VMEM((2, SEQ), jnp.int32), pltpu.VMEM((1, WIDTH), F32),
            pltpu.VMEM((2, SEQ, WIDTH), BF16),
            stream, stream, stream, stream,
            pltpu.VMEM((WIDTH, 2 * HEAD), BF16),
            stream, stream,
            pltpu.VMEM((SEQ, 2 * HEAD), BF16), pltpu.VMEM((SEQ, 2 * HEAD), BF16),
            pltpu.VMEM((HEAD, wide), F32), pltpu.VMEM((HEAD, wide), BF16), pltpu.VMEM((HEAD, wide), BF16),
            pltpu.VMEM((SEQ, 2 * HEAD), F32), pltpu.VMEM((SEQ, WIDTH), F32),
            pltpu.VMEM((TENSOR, 2, SEQ), F32), pltpu.VMEM((TENSOR, 1, SEQ), F32),
            pltpu.VMEM((1, SEQ), F32), pltpu.VMEM((1, SEQ), F32),
            dma((7,)), dma((parts,)), dma((parts,)), dma((parts,)), dma((parts,)),
            dma((TENSOR - 1,)), dma((TENSOR,)), dma((TENSOR - 1,)), dma((TENSOR,)), dma, dma,
            regular, regular, regular, regular, regular, regular,
            held, held, dma((2,)), dma((2,)), dma((2,)), dma((2,)),
        ],
        compiler_params=pltpu.CompilerParams(collective_id=0, has_side_effects=True, vmem_limit_bytes=24 << 20),
    )(*[pltpu.with_memory_space_constraint(a, pltpu.HBM) for a in (batch_order, segment_ids, produced[0], upstream[0], saved_inputs[0], norm_gain, w_key[0, 0], w_value[0, 0])])
    forward_out, input_grad = pl.pallas_call(
        write_out,
        out_shape=(rows, rows),
        in_specs=[vmem, vmem],
        out_specs=(hbm, hbm),
        scratch_shapes=[dma((2,))],
        compiler_params=pltpu.CompilerParams(vmem_limit_bytes=4 << 20),
    )(forward_out, input_grad)
    return forward_out[None], input_grad[None]


def solution(mesh):
    return jax.shard_map(
        on_device,
        mesh=mesh,
        in_specs=(
            P("section", None, None, "tensor"),
            P("section", None, "tensor"),
            P("section", None, "tensor"),
            P("section", "tensor"),
            P("section", "tensor", None, None),
            P("section", "tensor", None, None),
            P(),
            P(),
        ),
        out_specs=(P("section", None, "tensor"), P("section", None, "tensor")),
        check_vma=False,
    )
```

```python
import jax
import jax.numpy as jnp
from jax import lax
from jax.experimental import pallas as pl
from jax.experimental.pallas import tpu as pltpu
from jax.sharding import PartitionSpec as P

D = 8192
EPSILON = 1e-05
SECTIONS, TENSOR = 128, 8
SEQ, WIDTH, HEADS, HEAD = 192, 1024, 8, 128
SCALE = HEAD**-0.5
MESH = pl.DeviceIdType.MESH
F32, BF16 = jnp.float32, jnp.bfloat16
CHUNKS = ((0, 128), (128, 64))
PATHS, FIRST = 6, 8
PIECES = tuple((i * 16, 16) for i in range(2 * PATHS))
PATH_OF = tuple(range(PATHS)) + tuple((i + PATHS - 2) % PATHS for i in range(PATHS))
HELD = ((0, 16), (16, 16))
X_RELAYS, G_RELAYS = (7, 6, 1, 5, 2), (0, 1, 6, 2, 5)
NEAR = 3

UNITS = tuple((0, 128, (h,), 0) for h in range(HEADS)) + tuple(
    (q, 32, tuple(range(h, h + 4)), q - 96) for q in (128, 160) for h in (0, 4)
)
GROUPS = ((0, tuple(range(0, 8))), (32, (8, 9)), (64, (10, 11)))


def dot(a, b, over, precision=None):
    return lax.dot_general(a, b, ((over[:1], over[1:]), ((), ())), precision=precision, preferred_element_type=F32)


def take(ref, unit):
    q, n, heads, _ = unit
    parts = [ref[q : q + n, h * HEAD : (h + 1) * HEAD] for h in heads]
    return parts[0] if len(parts) == 1 else jnp.concatenate(parts, axis=0)


def put(ref, unit, value):
    q, n, heads, _ = unit
    for i, h in enumerate(heads):
        ref[q : q + n, h * HEAD : (h + 1) * HEAD] = value[i * n : (i + 1) * n]


def as_row(columns):
    return jnp.sum(jnp.transpose(columns), axis=0, keepdims=True)


def as_columns(row):
    return jnp.transpose(jnp.broadcast_to(row, (HEAD, SEQ)))


def fold(wide):
    total = wide[:, 0:HEAD]
    for h in range(1, HEADS):
        total = total + wide[:, h * HEAD : (h + 1) * HEAD]
    return total


def masks_of(segment):
    counts = [jnp.sum(jnp.where(segment < v, 1.0, 0.0), axis=1, keepdims=True) for v in (1, 2, 3)]
    start = jnp.where(segment >= 3, counts[2], jnp.where(segment >= 2, counts[1], jnp.where(segment >= 1, counts[0], 0.0)))
    key = lax.broadcasted_iota(jnp.int32, (HEAD, HEAD), 0).astype(F32)
    lane = lax.broadcasted_iota(jnp.int32, (HEAD, HEAD), 1)
    masks = {}
    query = lane.astype(F32)
    masks[0] = (key <= query) & (key >= start[:, 0:HEAD])
    tail = jnp.broadcast_to(start[:, HEAD:SEQ], (8, SEQ - HEAD)).astype(BF16)
    place = lax.broadcasted_iota(jnp.int32, (SEQ - HEAD, HEAD), 0)
    lanes = lax.broadcasted_iota(jnp.int32, (SEQ - HEAD, HEAD), 1)
    for q in (128, 160):
        pick = jnp.where(place == lax.rem(lanes, 32) + (q - 128), 1.0, 0.0).astype(BF16)
        first = dot(tail, pick, (1, 0))[0:1]
        query = (lax.rem(lane, 32) + q).astype(F32)
        keys = key + (q - 96)
        masks[q] = (keys <= query) & (keys >= first)
    return masks


def normalized(ref, out, rows, scale, gain):
    q, n = rows
    for h in range(HEADS):
        at = slice(h * HEAD, (h + 1) * HEAD)
        out[q : q + n, at] = (ref[q : q + n, at].astype(F32) * scale[q : q + n] * gain[:, at]).astype(BF16)


def weights_of(unit, normed, keys, mask):
    koff = unit[3]
    scores = dot(keys[koff : koff + HEAD, 0:HEAD], take(normed, unit), (1, 1)) * SCALE
    scores = jnp.where(mask, scores, -jnp.inf)
    grown = jnp.exp(scores - jnp.max(scores, axis=0, keepdims=True))
    return grown * (1.0 / jnp.sum(grown, axis=0, keepdims=True))


def kernel(
    order_hbm, segments_hbm, produced, gs, ys, gain_hbm, wk_hbm, wv_hbm,
    fwd_out, bwd_out,
    order, segments, gain_ref, pair, xs, xin, gin, y, w, nx, ny, kvx, kvy, pt, pbt, dst, dkv, dn,
    stat, cstat, xstat, xstat_in,
    load_sem, xsend, xrecv, gsend, grecv, ssend, srecv, csend, crecv, tsend, trecv,
    peer_in, next_in, previous_in, x_relay_in, g_relay_in, g_target_in,
    x_held, g_held, x_held_recv, g_held_recv, x_held_send, g_held_send,
):
    s, t = lax.axis_index("section"), lax.axis_index("tensor")
    nxt, prv = (lax.rem(s + 1, SECTIONS), t), (lax.rem(s + SECTIONS - 1, SECTIONS), t)
    peers = [(s, lax.rem(t + d, TENSOR)) for d in range(1, TENSOR)]
    place = lax.rem(s, 16)
    x, block = lax.rem(s, 8), s // 8
    late = lax.rem(block, 2) == 1

    def partner(b):
        return b + 1 - 2 * lax.rem(b, 2)

    def relays(b, columns):
        return [(partner(b) * 8 + column, t) for column in columns]

    x_path = sum(jnp.where(x == column, path + 1, 0) for path, column in enumerate(X_RELAYS))
    g_path = sum(jnp.where(x == column, path + 1, 0) for path, column in enumerate(G_RELAYS))
    x_source, x_target = (partner(block) * 8 + 7, t), (lax.rem(partner(block) * 8 + 8, SECTIONS), t)
    g_source, g_target = (partner(block) * 8, t), (lax.rem(partner(block) * 8 + SECTIONS - 1, SECTIONS), t)

    def signal(semaphore, device):
        pl.semaphore_signal(semaphore, inc=1, device_id=device, device_id_type=MESH)

    barrier = pltpu.get_barrier_semaphore()
    for d in range(TENSOR - 1):
        pl.when(t + d + 1 < TENSOR)(lambda d=d: signal(barrier, peers[d]))
    pl.when(place != 15)(lambda: signal(barrier, nxt))
    pl.when(place == 0)(lambda: signal(barrier, prv))

    def greet(devices):
        for device in devices:
            signal(barrier, device)

    pl.when((x_path > 0) & jnp.logical_not(late))(lambda: greet([x_source]))
    pl.when((g_path > 0) & jnp.logical_not(late))(lambda: greet([g_source]))
    pl.when(place == 7)(lambda: greet(relays(block, X_RELAYS)))
    pl.when(place == 0)(lambda: greet(relays(block, G_RELAYS)))
    pl.when(x == 0)(lambda: greet(relays(lax.rem(s + SECTIONS - 1, SECTIONS) // 8, X_RELAYS)))
    pl.when((g_path > 0) & (g_path <= NEAR))(lambda: greet([g_target]))
    pl.when(x == 7)(lambda: greet(relays(lax.rem(s + 1, SECTIONS) // 8, G_RELAYS[NEAR:])))
    loads = [
        pltpu.make_async_copy(produced, pair, load_sem.at[0]),
        pltpu.make_async_copy(order_hbm, order, load_sem.at[1]),
        pltpu.make_async_copy(ys, y, load_sem.at[2]),
        pltpu.make_async_copy(wk_hbm, w.at[:, 0:HEAD], load_sem.at[3]),
        pltpu.make_async_copy(wv_hbm, w.at[:, HEAD : 2 * HEAD], load_sem.at[4]),
        pltpu.make_async_copy(segments_hbm, segments, load_sem.at[5]),
        pltpu.make_async_copy(gain_hbm, gain_ref, load_sem.at[6]),
    ]
    for load in loads:
        load.start()
    x_role, g_role = jnp.where(x_path > 0, 1, 0), jnp.where(g_path > 0, 1, 0)
    greeted = (
        t + jnp.where(place != 0, 1, 0) + jnp.where(place == 15, 1 + len(X_RELAYS), 0) + jnp.where(place == 8, len(G_RELAYS), 0)
        + jnp.where(x == 7, NEAR, 0) + jnp.where(g_path > NEAR, 1, 0) + x_role + jnp.where(late, x_role + g_role, 0)
    )
    pl.when(greeted > 0)(lambda: pl.semaphore_wait(barrier, greeted))
    pl.when(place != 0)(lambda: signal(next_in, prv))
    pl.when(place == 15)(lambda: signal(previous_in, nxt))

    @pl.when(x == 7)
    def _():
        for device in relays(lax.rem(s + 1, SECTIONS) // 8, G_RELAYS[:NEAR]):
            signal(g_target_in, device)

    pl.when((x_path > 0) & late)(lambda: signal(x_relay_in, x_source))
    pl.when((g_path > 0) & late)(lambda: signal(g_relay_in, g_source))
    for d in range(TENSOR - 1):
        pl.when(t + d + 1 >= TENSOR)(lambda d=d: signal(peer_in, peers[d]))

    def remote(src, dst, send, recv, device):
        return pltpu.make_async_remote_copy(
            src_ref=src, dst_ref=dst, send_sem=send, recv_sem=recv, device_id=device, device_id_type=MESH
        )

    def straight(i, src, dst, send, recv, device):
        q, n = PIECES[i]
        return remote(src.at[pl.ds(q, n)], dst.at[pl.ds(q, n)], send.at[i], recv.at[i], device)

    def to_relay(i, src, held, send, recv, device):
        (q, n), (at, _) = PIECES[i], HELD[i // PATHS]
        return remote(src.at[pl.ds(q, n)], held.at[pl.ds(at, n)], send.at[i], recv.at[i // PATHS], device)

    def from_relay(j, path, held, dst, send, recv, device):
        at, n = HELD[j]
        piece = PATHS + lax.rem(path + 2, PATHS) if j else path
        rows = pl.ds(pl.multiple_of(piece * n, 16), n)
        return remote(held.at[pl.ds(at, n)], dst.at[rows], send.at[j], recv.at[piece], device)

    g_copies = [straight(i, gs, gin, gsend, grecv, prv) for i in range(len(PIECES))]
    x_copies = [straight(i, xs, xin, xsend, xrecv, nxt) for i in range(len(PIECES))]
    g_devices, x_devices = relays(block, G_RELAYS), relays(block, X_RELAYS)
    g_split = [
        to_relay(i, gs, g_held, gsend, g_held_recv, g_devices[p - 1]) if p else g_copies[i] for i, p in enumerate(PATH_OF)
    ]
    x_split = [
        to_relay(i, xs, x_held, xsend, x_held_recv, x_devices[p - 1]) if p else x_copies[i] for i, p in enumerate(PATH_OF)
    ]
    x_total = remote(xstat, xstat_in, tsend, trecv, nxt)

    def start(copies):
        for copy in copies:
            copy.start()

    pl.when((x != 0) & (place != 15))(lambda: start(g_copies))
    pl.when(place == 8)(lambda: start(g_split))

    def serve(j, path, held, held_recv, held_send, dst, recv, target):
        at, n = HELD[j]
        remote(held.at[pl.ds(at, n)], held.at[pl.ds(at, n)], held_send.at[j], held_recv.at[j], target).wait_recv()
        from_relay(j, path, held, dst, held_send, recv, target).start()

    def serve_g():
        pl.when(g_path <= NEAR)(lambda: pl.semaphore_wait(g_target_in, 1))
        for j in range(2):
            serve(j, g_path, g_held, g_held_recv, g_held_send, gin, grecv, g_target)

    def serve_x(j):
        serve(j, x_path, x_held, x_held_recv, x_held_send, xin, xrecv, x_target)

    own_first = (place == 0) & (s != 0)

    loads[0].wait()
    loads[1].wait()
    wanted = order[lax.rem(s + 1, SECTIONS)]
    xs[...] = pair[wanted]

    pl.when(place == 15)(lambda: start(x_split + g_copies))

    @pl.when(x != 7)
    def _():
        pl.semaphore_wait(next_in, 1)
        start(x_copies[:FIRST])

    loads[2].wait()

    def squares(ref):
        total = None
        for h in range(HEADS):
            part = ref[:, h * HEAD : (h + 1) * HEAD].astype(F32)
            total = part * part if total is None else total + part * part
        return as_row(total)

    stat[t, 0:1, :] = squares(y)
    stat[t, 1:2, :] = squares(xs)

    def to_peers(box, send, recv):
        return [remote(box.at[t], box.at[t], send.at[d], recv.at[t], peers[d]) for d in range(TENSOR - 1)]

    def from_peers(box, send, recv):
        for d in range(TENSOR - 1):
            slot = lax.rem(t + d + 1, TENSOR)
            remote(box.at[slot], box.at[slot], send.at[d], recv.at[slot], peers[d]).wait_recv()

    pl.when(t < TENSOR - 1)(lambda: pl.semaphore_wait(peer_in, TENSOR - 1 - t))
    stat_sends = to_peers(stat, ssend, srecv)
    start(stat_sends)

    for load in loads[3:]:
        load.wait()
    gain = gain_ref[...]
    forward = order[s].astype(F32)
    segment = segments[...].astype(F32)
    masks_b = masks_of(segment[1:2] + forward * (segment[0:1] - segment[1:2]))
    masks_f = masks_of(segment[0:1] + forward * (segment[1:2] - segment[0:1]))

    from_peers(stat, ssend, srecv)
    totals = jnp.sum(stat[...], axis=0)
    xstat[...] = totals[1:2]

    pl.when(x != 7)(lambda: start([x_total] + x_copies[FIRST:]))
    pl.when(place == 15)(lambda: start([x_total]))

    scale_row = lax.rsqrt(totals[0:1] / D + EPSILON)
    scale = as_columns(scale_row)
    normalized(y, ny, (0, SEQ), scale, gain)
    kvy[...] = dot(ny[...], w[...], (1, 0)).astype(BF16)
    for u, unit in enumerate(UNITS):
        p = weights_of(unit, ny, kvy, masks_b[unit[0]])
        pt[:, u * HEAD : (u + 1) * HEAD] = p
        pbt[:, u * HEAD : (u + 1) * HEAD] = p.astype(BF16)

    @pl.when(place == 0)
    def _():
        pl.semaphore_wait(previous_in, 1)
        pl.semaphore_wait(g_relay_in, len(G_RELAYS))
        start(g_split)

    @pl.when(place == 7)
    def _():
        pl.semaphore_wait(next_in, 1)
        pl.semaphore_wait(x_relay_in, len(X_RELAYS))
        start([x_total] + x_split)

    def backward(units):
        for u in units:
            unit, at = UNITS[u], slice(u * HEAD, (u + 1) * HEAD)
            koff = unit[3]
            dp = dot(kvy[koff : koff + HEAD, HEAD : 2 * HEAD], take(gin, unit), (1, 1))
            p = pt[:, at]
            rows = jnp.sum(dp * p, axis=0, keepdims=True)
            ds = (p * (dp - rows) * SCALE).astype(BF16)
            dst[:, at] = ds
            put(dn, unit, dot(ds, kvy[koff : koff + HEAD, 0:HEAD], (0, 0)))

    def key_grads(group):
        koff, units = group
        at = slice(units[0] * HEAD, (units[-1] + 1) * HEAD)
        grads = jnp.concatenate([take(gin, UNITS[u]) for u in units], axis=0)
        queries = jnp.concatenate([take(ny, UNITS[u]) for u in units], axis=0)
        dkv[koff : koff + HEAD, 0:HEAD] += dot(dst[:, at], queries, (1, 0))
        dkv[koff : koff + HEAD, HEAD : 2 * HEAD] += dot(pbt[:, at], grads, (1, 0))

    dkv[...] = jnp.zeros_like(dkv)
    pl.when((g_path > 0) & jnp.logical_not(own_first))(serve_g)
    pl.when(x == 7)(lambda: serve_x(0))
    for copy in g_copies[:FIRST]:
        copy.wait_recv()
    backward(GROUPS[0][1])
    key_grads(GROUPS[0])
    pl.when((x_path > 0) & (x != 7))(lambda: serve_x(0))
    pl.when(x_path > 0)(lambda: serve_x(1))
    for copy in g_copies[FIRST:]:
        copy.wait_recv()
    for group in GROUPS[1:]:
        backward(group[1])
        key_grads(group)
    rounded = dkv[...].astype(BF16)
    total = None
    for h in range(HEADS):
        at = slice(h * HEAD, (h + 1) * HEAD)
        d = dn[:, at] + dot(rounded, w[at, :], (1, 1))
        scaled = d * gain[:, at]
        dn[:, at] = gin[:, at].astype(F32) + scale * scaled
        part = scaled * y[:, at].astype(F32)
        total = part if total is None else total + part
    cstat[t, 0:1, :] = as_row(total)
    c_sends = to_peers(cstat, csend, crecv)
    start(c_sends)
    pl.when(own_first)(serve_g)

    def finish_backward():
        from_peers(cstat, csend, crecv)
        inner = jnp.sum(cstat[...], axis=0)
        pull = as_columns(scale_row * scale_row * scale_row / D * inner)
        for h in range(HEADS):
            at = slice(h * HEAD, (h + 1) * HEAD)
            bwd_out[:, at] = (dn[:, at] - y[:, at].astype(F32) * pull).astype(BF16)

    finish_first = (x == 0) & (s != 0)
    pl.when(finish_first)(finish_backward)

    for copy in x_copies[:FIRST]:
        copy.wait_recv()
    x_total.wait_recv()
    scale_f = as_columns(lax.rsqrt(xstat_in[...] / D + EPSILON))
    for i, (q, n) in enumerate(CHUNKS):
        if i:
            for copy in x_copies[FIRST:]:
                copy.wait_recv()
        normalized(xin, nx, (q, n), scale_f, gain)
        kvx[q : q + n] = dot(nx[q : q + n], w[...], (1, 0)).astype(BF16)
        for unit in UNITS:
            if q <= unit[0] < q + n:
                koff = unit[3]
                p = weights_of(unit, nx, kvx, masks_f[unit[0]]).astype(BF16)
                mixed = dot(p, kvx[koff : koff + HEAD, HEAD : 2 * HEAD], (0, 0)).astype(BF16).astype(F32)
                put(fwd_out, unit, (take(xin, unit).astype(F32) + mixed).astype(BF16))

    pl.when(jnp.logical_not(finish_first))(finish_backward)

    for copy in stat_sends + g_copies + x_copies + [x_total] + c_sends:
        copy.wait_send()
    for path, held, held_send, dst, recv, target in (
        (g_path, g_held, g_held_send, gin, grecv, g_target),
        (x_path, x_held, x_held_send, xin, xrecv, x_target),
    ):

        @pl.when(path > 0)
        def _(path=path, held=held, held_send=held_send, dst=dst, recv=recv, target=target):
            for j in range(2):
                from_relay(j, path, held, dst, held_send, recv, target).wait_send()


def write_out(first, second, first_out, second_out, semaphore):
    copies = [pltpu.make_async_copy(first, first_out, semaphore.at[0]), pltpu.make_async_copy(second, second_out, semaphore.at[1])]
    for copy in copies:
        copy.start()
    for copy in copies:
        copy.wait()


def on_device(produced, saved_inputs, upstream, norm_gain, w_key, w_value, batch_order, segment_ids):
    rows = jax.ShapeDtypeStruct((SEQ, WIDTH), BF16)
    hbm, vmem = pl.BlockSpec(memory_space=pltpu.HBM), pl.BlockSpec(memory_space=pltpu.VMEM)
    stream = pltpu.VMEM((SEQ, WIDTH), BF16)
    wide = len(UNITS) * HEAD
    dma, regular = pltpu.SemaphoreType.DMA, pltpu.SemaphoreType.REGULAR
    parts = len(PIECES)
    held = pltpu.VMEM((32, WIDTH), BF16)
    forward_out, input_grad = pl.pallas_call(
        kernel,
        out_shape=(rows, rows),
        in_specs=[hbm] * 8,
        out_specs=(vmem, vmem),
        scratch_shapes=[
            pltpu.SMEM((SECTIONS,), jnp.int32), pltpu.VMEM((2, SEQ), jnp.int32), pltpu.VMEM((1, WIDTH), F32),
            pltpu.VMEM((2, SEQ, WIDTH), BF16),
            stream, stream, stream, stream,
            pltpu.VMEM((WIDTH, 2 * HEAD), BF16),
            stream, stream,
            pltpu.VMEM((SEQ, 2 * HEAD), BF16), pltpu.VMEM((SEQ, 2 * HEAD), BF16),
            pltpu.VMEM((HEAD, wide), F32), pltpu.VMEM((HEAD, wide), BF16), pltpu.VMEM((HEAD, wide), BF16),
            pltpu.VMEM((SEQ, 2 * HEAD), F32), pltpu.VMEM((SEQ, WIDTH), F32),
            pltpu.VMEM((TENSOR, 2, SEQ), F32), pltpu.VMEM((TENSOR, 1, SEQ), F32),
            pltpu.VMEM((1, SEQ), F32), pltpu.VMEM((1, SEQ), F32),
            dma((7,)), dma((parts,)), dma((parts,)), dma((parts,)), dma((parts,)),
            dma((TENSOR - 1,)), dma((TENSOR,)), dma((TENSOR - 1,)), dma((TENSOR,)), dma, dma,
            regular, regular, regular, regular, regular, regular,
            held, held, dma((2,)), dma((2,)), dma((2,)), dma((2,)),
        ],
        compiler_params=pltpu.CompilerParams(collective_id=0, has_side_effects=True, vmem_limit_bytes=24 << 20),
    )(*[pltpu.with_memory_space_constraint(a, pltpu.HBM) for a in (batch_order, segment_ids, produced[0], upstream[0], saved_inputs[0], norm_gain, w_key[0, 0], w_value[0, 0])])
    forward_out, input_grad = pl.pallas_call(
        write_out,
        out_shape=(rows, rows),
        in_specs=[vmem, vmem],
        out_specs=(hbm, hbm),
        scratch_shapes=[dma((2,))],
        compiler_params=pltpu.CompilerParams(vmem_limit_bytes=4 << 20),
    )(forward_out, input_grad)
    return forward_out[None], input_grad[None]


def solution(mesh):
    return jax.shard_map(
        on_device,
        mesh=mesh,
        in_specs=(
            P("section", None, None, "tensor"),
            P("section", None, "tensor"),
            P("section", None, "tensor"),
            P("section", "tensor"),
            P("section", "tensor", None, None),
            P("section", "tensor", None, None),
            P(),
            P(),
        ),
        out_specs=(P("section", None, "tensor"), P("section", None, "tensor")),
        check_vma=False,
    )
```
